512 devices in a mesh: lat: 64 (over y_lo, x, z), lon: 8 (over y_hi, core).
Axes of the slice: x: 4, y: 8 (y_hi: 4, y_lo: 2; y = y_hi * 2 + y_lo), z: 8, core: 2. Of those that a mesh axis runs over, the one named last changes fastest.
Arguments:
- coefficients: float32 [256, 2, 3, 2, 513], P('lat'), may hold values from -0.03125 to 0.03125
- pair_orders: int32 [256], replicated, may hold values from 0 to 255, each once
Outputs:
- potential: float32 [3, 2, 1024, 2048], P(None, None, 'lat', 'lon')
- magnetic_field: float32 [3, 2, 1024, 2048], P(None, None, 'lat', 'lon')
The draws below stay inside these ranges and needn't reach their ends.
Inputs may be any that keep to these rules, and one draw needn't show every extreme that they name: A permutation of 0 to 255; row p of coefficients holds the orders pair_orders[p] and 511 - pair_orders[p].
All inputs are finite; a program needn't handle non-finite values.
Results may differ from the reference program's by a relative error of at most 0.0003.
Values sent between devices are 32-bit elements; how exact they have to be, the bound alone decides.
No kernel may reach another device: no remote copies, remote signals or barrier semaphores. Data moves between devices by JAX's collectives and lax.ppermute only.
A program may use at most 64 MiB of HBM per device.

```python
import math
import jax
import jax.numpy as jnp
from jax import lax

ORDERS = 512
NT = 1024
NP = 2048
R = 2
STEPS = 2
PAIRS = 256
SROWS = 513


def steps_of(key, shape, shards, least, largest):
    factor_of = 1.0
    for axis_at, blocks in shards:
        draws = jax.random.uniform(jax.random.fold_in(jax.random.fold_in(key, 6), axis_at), (blocks,), jnp.float32, least / len(shards), largest / len(shards))
        factor_of = factor_of * jnp.repeat(jnp.exp(draws), shape[axis_at] // blocks).reshape((-1,) + (1,) * (len(shape) - 1 - axis_at))
    return factor_of


def scatter_about(key, dims, spread, most, shards=(), kind=jnp.bfloat16):
    entries = jax.random.normal(key, dims, jnp.float32) * spread
    if len(shards) > 0:
        entries = steps_of(key, dims, shards, -0.22, 0.18) * entries
    return jnp.clip(entries, min=-most, max=most).astype(kind)


def setup_inputs(seed: int = 0) -> dict:
    key_of = jax.random.split(jax.random.key(seed), 3)
    coefficients = scatter_about(key_of[0], (PAIRS, 2, 3, R, SROWS), (3.0 / ORDERS), 0.03125, ((0, 64),), jnp.float32)
    pair_orders = jax.random.permutation(key_of[1], PAIRS).astype(jnp.int32)
    return {"coefficients": coefficients, "pair_orders": pair_orders}


soft_floor = 1.0
resist = 0.2
time_step = 0.3
rescale_at = 10000000000.0
block_steps = 64
span_start = math.pi / 6.0
span_width = 2.0 * math.pi / 3.0

def row_angles(row_ids, row_total):
    return span_start + (row_ids.astype(jnp.float32) + 0.5) * (span_width / row_total)

def norm_logs(order_total):
    degrees = jnp.arange(1, order_total, dtype=jnp.float32)
    log_terms = 0.5 * jnp.log((2.0 * degrees + 1.0) / (2.0 * degrees))
    return jnp.concatenate([jnp.zeros((1,), jnp.float32), jnp.cumsum(log_terms)]) - 0.5 * jnp.log(4.0 * math.pi)

def pick_logs(log_table, orders):
    order_grid = jnp.arange(log_table.shape[0], dtype=jnp.int32)
    return lax.optimization_barrier(jnp.sum(jnp.where(order_grid[None, :] == orders[:, None], log_table[None, :], 0.0), axis=1))

def synthesize(coef_rows, small_orders, angles, order_total):
    pair_count = coef_rows.shape[0]
    columns = coef_rows.shape[1] * coef_rows.shape[2] * coef_rows.shape[3]
    packed = coef_rows.shape[4]
    block_count = -(-packed // block_steps)
    padded = block_count * block_steps
    flat_coef = jnp.pad(coef_rows.reshape(pair_count, columns, packed), ((0, 0), (0, 0), (0, padded - packed)))
    large_orders = order_total - 1 - small_orders
    low_order = small_orders.astype(jnp.float32)
    high_order = large_orders.astype(jnp.float32)
    switch = order_total - low_order
    positions = jnp.arange(padded, dtype=jnp.float32)
    low_mask = (positions[None, :] < switch[:, None]).astype(jnp.float32)
    masked = flat_coef[:, None, :, :] * jnp.stack([low_mask, 1.0 - low_mask], axis=1)[:, :, None, :]
    log_table = norm_logs(order_total)
    log_sin = jnp.log(jnp.sin(angles))
    cosine = jnp.cos(angles)
    seed_low = pick_logs(log_table, small_orders)[:, None] + low_order[:, None] * log_sin[None, :]
    seed_high = pick_logs(log_table, large_orders)[:, None] + high_order[:, None] * log_sin[None, :]
    log_big = math.log(rescale_at)

    def advance(carried, step_now):
        previous, current, scaling = carried
        low_side = step_now < switch
        order_now = jnp.where(low_side, low_order, high_order)
        degree = jnp.where(low_side, low_order + step_now, step_now - 1.0)
        starting = (degree == order_now)[:, None]
        factor = jnp.sqrt(jnp.maximum(4.0 * degree * degree - 1.0, 1.0) / jnp.maximum(degree * degree - order_now * order_now, 1.0))
        prior_degree = degree - 1.0
        back_factor = jnp.where(prior_degree > order_now, jnp.sqrt((prior_degree * prior_degree - order_now * order_now) / jnp.maximum(4.0 * prior_degree * prior_degree - 1.0, 1.0)), 0.0)
        next_value = factor[:, None] * (cosine[None, :] * current - back_factor[:, None] * previous)
        seed_now = jnp.where(low_side[:, None], seed_low, seed_high)
        previous = jnp.where(starting, 0.0, current)
        current = jnp.where(starting, 1.0, next_value)
        scaling = jnp.where(starting, seed_now, scaling)
        too_big = jnp.abs(current) > rescale_at
        shrink = jnp.where(too_big, 1.0 / rescale_at, 1.0)
        previous = previous * shrink
        current = current * shrink
        scaling = scaling + jnp.where(too_big, log_big, 0.0)
        return ((previous, current, scaling), current * jnp.exp(scaling))

    def run_block(carried, block_index):
        rec_state, synth_sum = carried
        step_values = block_index.astype(jnp.float32) * block_steps + jnp.arange(block_steps, dtype=jnp.float32)
        rec_state, values = lax.scan(advance, rec_state, step_values, unroll=8)
        coef_block = lax.dynamic_slice_in_dim(masked, block_index * block_steps, block_steps, 3)
        synth_sum = synth_sum + jnp.einsum('spt,pkcs->pkct', values, coef_block, precision=lax.Precision.HIGHEST, preferred_element_type=jnp.float32)
        return ((rec_state, synth_sum), None)
    zero_rows = jnp.zeros((pair_count, angles.shape[0]), jnp.float32)
    zero_sum = jnp.zeros((pair_count, 2, columns, angles.shape[0]), jnp.float32)
    scanned = lax.scan(run_block, ((zero_rows, zero_rows, zero_rows), zero_sum), jnp.arange(block_count, dtype=jnp.int32))
    synth_sum = scanned[0][1]
    return synth_sum.reshape(pair_count * 2, 2, columns // 2, angles.shape[0])

def sector_table(slot_orders, column_start, col_count, point_total):
    column_ids = column_start + jnp.arange(col_count, dtype=jnp.int32)
    turn_count = slot_orders[:, None] * column_ids[None, :] % point_total
    phase_angle = turn_count.astype(jnp.float32) * (2.0 * math.pi / point_total)
    return jnp.stack([jnp.cos(phase_angle), jnp.sin(phase_angle)], axis=1)

def transform(rows_part, sector_basis):
    return jnp.einsum('gxcr,gxf->crf', rows_part, sector_basis, precision=lax.Precision.HIGHEST, preferred_element_type=jnp.float32)

def curl(padded, row_sin, phi_ratio):
    center = padded[:, :, 1:-1, 1:-1]
    theta_diff = 0.5 * (padded[:, :, 2:, 1:-1] - padded[:, :, :-2, 1:-1])
    phi_scale = (1.0 / (2.0 * phi_ratio * row_sin))[None, :, None]
    lifted = jnp.pad(center, ((0, 0), (1, 1), (0, 0), (0, 0)))
    radial_diff = 0.5 * (lifted[:, 2:] - lifted[:, :-2])
    phi_radial = (padded[0, :, 1:-1, 2:] - padded[0, :, 1:-1, :-2]) * phi_scale
    phi_theta = (padded[1, :, 1:-1, 2:] - padded[1, :, 1:-1, :-2]) * phi_scale
    return jnp.stack([theta_diff[2] - phi_theta, phi_radial - radial_diff[2], radial_diff[1] - theta_diff[0]])

def cross_product(first_vec, second_vec):
    return jnp.stack([first_vec[1] * second_vec[2] - first_vec[2] * second_vec[1], first_vec[2] * second_vec[0] - first_vec[0] * second_vec[2], first_vec[0] * second_vec[1] - first_vec[1] * second_vec[0]])

def drift(magnetic, current):
    lorentz = cross_product(current, magnetic)
    velocity = lorentz / (lax.optimization_barrier(jnp.sum(magnetic * magnetic, axis=0)) + soft_floor)
    return cross_product(velocity, magnetic) - resist * current

def extend_grid(values):
    taller = jnp.pad(values, ((0, 0), (0, 0), (1, 1), (0, 0)))
    return jnp.concatenate([taller[..., -1:], taller, taller[..., :1]], axis=3)

def reference(coefficients, pair_orders):
    order_total = 2 * PAIRS
    angles = row_angles(jnp.arange(NT, dtype=jnp.int32), NT)
    spectral = synthesize(coefficients, pair_orders, angles, order_total)
    slot_orders = jnp.stack([pair_orders, order_total - 1 - pair_orders], axis=1).reshape(order_total)
    potential = transform(spectral, sector_table(slot_orders, 0, NP, NP)).reshape(3, R, NT, NP)
    sin_rows = jnp.sin(angles)
    phi_ratio = 3.0 * NT / NP
    magnetic = potential
    for step_now in range(STEPS):
        magnetic = curl(extend_grid(potential), sin_rows, phi_ratio)
        current = curl(extend_grid(magnetic), sin_rows, phi_ratio)
        potential = potential + time_step * drift(magnetic, current)
    return (potential, magnetic)
```

```python
import math

import jax
import jax.numpy as jnp
import numpy as np
from jax import lax
from jax.experimental import pallas as pl
from jax.experimental.pallas import tpu as pltpu
from jax.sharding import PartitionSpec as P

ORDERS = 512
NT = 1024
NP = 2048
STEPS = 2
LAT = 64
LON = 8
BAND = NT // LAT
SECTOR = NP // LON
HALO = 4
EXT = BAND + 2 * HALO
PAIRS_LOCAL = 4
HALF = LAT // 2
CHUNKS = 18
COLS = SECTOR + 16

soft_floor = 1.0
resist = 0.2
time_step = 0.3
rescale_at = 1.0e10
block_steps = 16
span_start = math.pi / 6.0
span_width = 2.0 * math.pi / 3.0

EXCHANGE = list(range(HALF)) + [LAT - 1 - u for u in range(HALF)]


def geometry():
    rows = (
        BAND * np.arange(HALF)[None, None, :]
        + 8 * np.arange(2)[:, None, None]
        + np.arange(8)[None, :, None]
    )
    theta = span_start + (rows + 0.5) * (span_width / NT)
    cosine = np.tile(np.cos(theta), (1, 1, PAIRS_LOCAL))
    log_sin = np.tile(np.log(np.sin(theta)), (1, 1, PAIRS_LOCAL))
    return np.concatenate([cosine, log_sin]).astype(np.float32)


def norm_logs():
    k = np.arange(1, ORDERS, dtype=np.float64)
    logs = np.concatenate([[0.0], np.cumsum(0.5 * np.log((2 * k + 1) / (2 * k)))])
    return (logs - 0.5 * np.log(4 * np.pi)).astype(np.float32)


def split2(value):
    high = value.astype(jnp.bfloat16)
    low = (value - high.astype(jnp.float32)).astype(jnp.bfloat16)
    return high, low


def dot(a, b):
    return jnp.dot(a, b, preferred_element_type=jnp.float32)


def synth_kernel(
    order_ref, log_ref, geom_ref, coef_ref, out_ref,
    fac_ref, back_ref, leg_ref, coefs_ref, wh_ref, wl_ref, stack_ref, extra_ref,
):
    lane = lax.broadcasted_iota(jnp.int32, (8, 128), 1)
    pair_of_lane = lane // HALF
    unit = lane % HALF

    def per_pair(values):
        result = jnp.full((8, 128), values[0], values[0].dtype)
        for p in range(1, PAIRS_LOCAL):
            result = jnp.where(pair_of_lane == p, values[p], result)
        return result

    lows = [order_ref[p] for p in range(PAIRS_LOCAL)]
    low = per_pair([o.astype(jnp.float32) for o in lows])
    high = (ORDERS - 1.0) - low
    switch = ORDERS - low

    def factors(c, _):
        base = c * 8
        step = lax.broadcasted_iota(jnp.int32, (8, 128), 0).astype(jnp.float32) + base.astype(jnp.float32)
        low_side = step < switch
        order = jnp.where(low_side, low, high)
        degree = jnp.where(low_side, low + step, step - 1.0)
        prior = degree - 1.0
        order2 = order * order
        degree2 = degree * degree
        prior2 = prior * prior
        factor = jnp.sqrt(jnp.maximum(4.0 * degree2 - 1.0, 1.0) / jnp.maximum(degree2 - order2, 1.0))
        back = jnp.sqrt(jnp.maximum(prior2 - order2, 0.0) / jnp.maximum(4.0 * prior2 - 1.0, 1.0))
        fac_ref[pl.ds(pl.multiple_of(base, 8), 8), :] = factor
        back_ref[pl.ds(pl.multiple_of(base, 8), 8), :] = jnp.where(prior > order, factor * back, 0.0)
        return 0

    lax.fori_loop(0, 65, factors, 0)

    coefs_ref[...] = jnp.zeros_like(coefs_ref)
    for p in range(PAIRS_LOCAL):
        for x in range(2):
            for c in range(3):
                row = (p * 2 + x) * 8 + c * 2
                coefs_ref[row:row + 2, 0:513] = coef_ref[p, x, c]
    slot = lax.broadcasted_iota(jnp.int32, (8, 512), 1)
    for p in range(PAIRS_LOCAL):
        is_low = slot < ORDERS - lows[p]
        low_sign = 1.0 - 2.0 * (slot % 2).astype(jnp.float32)
        high_sign = 1.0 - 2.0 * ((slot + lows[p]) % 2).astype(jnp.float32)
        for x in range(2):
            row = (p * 2 + x) * 8
            both = coefs_ref[row:row + 8, 0:512]
            parts = [jnp.where(is_low, both, 0.0), jnp.where(is_low, 0.0, both)]
            for side in range(2):
                for h in range(2):
                    w = parts[h] if side == 0 else parts[h] * (low_sign if h == 0 else high_sign)
                    at = (((side * PAIRS_LOCAL + p) * 2 + h) * 2 + x) * 8
                    wh, wl = split2(w)
                    wh_ref[at:at + 8, :] = wh.astype(jnp.float32)
                    wl_ref[at:at + 8, :] = wl.astype(jnp.float32)

    cosine = [geom_ref[0], geom_ref[1]]
    log_sin = [geom_ref[2], geom_ref[3]]
    norm_low = per_pair([log_ref[o] for o in lows])
    norm_high = per_pair([log_ref[ORDERS - 1 - o] for o in lows])
    seed_low = [norm_low + low * log_sin[v] for v in range(2)]
    seed_high = [norm_high + high * log_sin[v] for v in range(2)]
    start_scale = [jnp.exp(seed_high[v]) for v in range(2)]
    log_big = math.log(rescale_at)

    def run(base, count, state, restart, first):
        state = [list(s) for s in state]
        for k in range(count):
            s = base + k
            fac = fac_ref[pl.ds(s, 1), :]
            back = back_ref[pl.ds(s, 1), :]
            if restart:
                starting = switch == (s.astype(jnp.float32) if not isinstance(s, int) else float(s))
            for v in range(2):
                previous, current, scaling, scale = state[v]
                if first and k == 0:
                    value = jnp.ones((8, 128), jnp.float32)
                else:
                    value = (fac * cosine[v]) * current - back * previous
                if restart:
                    value = jnp.where(starting, 1.0, value)
                    scaling = jnp.where(starting, seed_high[v], scaling)
                    scale = jnp.where(starting, start_scale[v], scale)
                state[v] = [current, value, scaling, scale]
                at = s * 8 if isinstance(s, int) else pl.multiple_of(s * 8, 8)
                leg_ref[v, pl.ds(at, 8), :] = value * scale
        for v in range(2):
            previous, current, scaling, scale = state[v]
            big = jnp.abs(current) > rescale_at
            shrink = jnp.where(big, 1.0 / rescale_at, 1.0)
            scaling = scaling + jnp.where(big, log_big, 0.0)
            state[v] = [previous * shrink, current * shrink, scaling, jnp.exp(scaling)]
        return tuple(tuple(s) for s in state)

    zero = jnp.zeros((8, 128), jnp.float32)
    state = tuple((zero, zero, seed_low[v], jnp.exp(seed_low[v])) for v in range(2))
    state = run(0, block_steps, state, False, True)
    state = lax.fori_loop(
        1, 16, lambda b, st: run(b * block_steps, block_steps, st, False, False), state
    )
    state = lax.fori_loop(
        16, 32, lambda b, st: run(b * block_steps, block_steps, st, True, False), state
    )
    run(512, 1, state, True, False)

    tail_sign = per_pair([1.0 - 2.0 * (o % 2).astype(jnp.float32) for o in lows])
    tails = []
    for x in range(2):
        tail = jnp.zeros((8, 128), jnp.float32)
        for p in range(PAIRS_LOCAL):
            row = (p * 2 + x) * 8
            column = jnp.broadcast_to(coefs_ref[row:row + 8, 512:513], (8, 128))
            tail = jnp.where(pair_of_lane == p, column, tail)
        tails.append(tail)
    wh = wh_ref[...].astype(jnp.bfloat16)
    wl = wl_ref[...].astype(jnp.bfloat16)
    for v in range(2):
        for t in range(0, 8, 2):
            values = jnp.concatenate(
                [leg_ref[v, pl.ds(t + d, 512, stride=8), :] for d in range(2)], axis=1
            )
            vh, vl = split2(values)
            summed = dot(wh, vh) + dot(wl, vh) + dot(wh, vl)
            for d in range(2):
                r = 8 * v + t + d
                last = leg_ref[v, pl.ds(512 * 8 + t + d, 1), :]
                part = summed[:, 128 * d:128 * d + 128]
                for side in range(2):
                    for h in range(2):
                        for x in range(2):
                            picked = None
                            for p in range(PAIRS_LOCAL):
                                at = (((side * PAIRS_LOCAL + p) * 2 + h) * 2 + x) * 8
                                block = part[at:at + 8, :]
                                picked = block if p == 0 else jnp.where(pair_of_lane == p, block, picked)
                            if h == 1:
                                term = tails[x] * last
                                picked = picked + (term if side == 0 else term * tail_sign)
                            e = HALO + (r if side == 0 else BAND - 1 - r)
                            stack_ref[(side * 2 + h) * 2 + x, 6 * e:6 * e + 6, :] = picked[0:6]

    wide_unit = lax.broadcasted_iota(jnp.int32, (24, 128), 1) % HALF
    for h in range(2):
        for x in range(2):
            north, south = h * 2 + x, 4 + h * 2 + x
            n_first, n_last = stack_ref[north, 24:48, :], stack_ref[north, 96:120, :]
            s_first, s_last = stack_ref[south, 24:48, :], stack_ref[south, 96:120, :]
            stack_ref[north, 0:24, :] = jnp.where(wide_unit == 0, 0.0, pltpu.roll(n_last, 1, 1))
            stack_ref[north, 120:144, :] = jnp.where(
                wide_unit == HALF - 1, s_first, pltpu.roll(n_first, 127, 1)
            )
            stack_ref[south, 0:24, :] = jnp.where(
                wide_unit == HALF - 1, n_last, pltpu.roll(s_last, 127, 1)
            )
            stack_ref[south, 120:144, :] = jnp.where(wide_unit == 0, 0.0, pltpu.roll(s_first, 1, 1))

    wide_lane = lax.broadcasted_iota(jnp.int32, (HALF, 128), 1)
    for side in range(2):
        for h in range(2):
            for x in range(2):
                which = (side * 2 + h) * 2 + x
                turned = stack_ref[which, 0:128, :].T
                for p in range(PAIRS_LOCAL):
                    chunk = (p * 2 + h) * 2 + x
                    out_ref[pl.ds(side * HALF * CHUNKS + chunk, HALF, stride=CHUNKS), :] = turned[
                        HALF * p:HALF * p + HALF, :
                    ]
                for copy in range(2):
                    at = copy * 64 + (h * 2 + x) * 16
                    extra_ref[at:at + 16, :] = stack_ref[which, 128:144, :]
        turned = extra_ref[...].T
        for q in range(2):
            first = turned[2 * q * HALF:2 * q * HALF + HALF, :]
            second = turned[(2 * q + 1) * HALF:(2 * q + 2) * HALF, :]
            out_ref[pl.ds(side * HALF * CHUNKS + 16 + q, HALF, stride=CHUNKS), :] = jnp.where(
                wide_lane < 64, first, second
            )


def synthesize(own_orders, coefficients):
    scratch = [
        pltpu.VMEM((520, 128), jnp.float32),
        pltpu.VMEM((520, 128), jnp.float32),
        pltpu.VMEM((2, 520 * 8, 128), jnp.float32),
        pltpu.VMEM((64, 640), jnp.float32),
        pltpu.VMEM((256, 512), jnp.float32),
        pltpu.VMEM((256, 512), jnp.float32),
        pltpu.VMEM((8, 144, 128), jnp.float32),
        pltpu.VMEM((128, 128), jnp.float32),
    ]
    return pl.pallas_call(
        synth_kernel,
        out_shape=jax.ShapeDtypeStruct((LAT * CHUNKS, 128), jnp.float32),
        in_specs=[
            pl.BlockSpec(memory_space=pltpu.SMEM),
            pl.BlockSpec(memory_space=pltpu.SMEM),
            pl.BlockSpec(memory_space=pltpu.VMEM),
            pl.BlockSpec(memory_space=pltpu.VMEM),
        ],
        out_specs=pl.BlockSpec(memory_space=pltpu.VMEM),
        scratch_shapes=scratch,
        compiler_params=pltpu.CompilerParams(vmem_limit_bytes=40 * 1024 * 1024),
        name="synthesis",
    )(own_orders, norm_logs(), geometry(), coefficients)


def relax_kernel(recv_ref, th_ref, tl_ref, rows_ref, pot_ref, mag_ref, dh_ref, dl_ref, turn_ref, plane_ref):
    for p in range(PAIRS_LOCAL):
        rest = recv_ref[pl.ds(16 + p // 2, LAT, stride=CHUNKS), :]
        for hx in range(4):
            chunk = p * 4 + hx
            main = recv_ref[pl.ds(chunk, LAT, stride=CHUNKS), :]
            offset = (p % 2) * 64 + hx * 16
            tail = pltpu.roll(rest, (128 - offset) % 128, 1) if offset else rest
            mh, ml = split2(main)
            eh, el = split2(tail)
            dh_ref[chunk * LAT:chunk * LAT + LAT, 0:128] = mh
            dl_ref[chunk * LAT:chunk * LAT + LAT, 0:128] = ml
            dh_ref[chunk * LAT:chunk * LAT + LAT, 128:256] = eh
            dl_ref[chunk * LAT:chunk * LAT + LAT, 128:256] = el
    dh, dl = dh_ref[...], dl_ref[...]
    th, tl = th_ref[...], tl_ref[...]
    turn_ref[0:COLS, :] = dot(th, dh) + dot(tl, dh) + dot(th, dl)
    turn_ref[COLS:, :] = jnp.zeros((384 - COLS, 256), jnp.float32)
    for j in range(3):
        plane_ref[j, 0:128, :] = turn_ref[128 * j:128 * j + 128, 0:128].T
        plane_ref[j, 128:256, :] = turn_ref[128 * j:128 * j + 128, 128:256].T
    planes = [
        jnp.concatenate([plane_ref[j, pl.ds(cr, EXT, stride=6), :] for j in range(3)], axis=1)
        for cr in range(6)
    ]
    field = [[planes[c * 2 + r] for r in range(2)] for c in range(3)]
    scale = jnp.concatenate([rows_ref[0]] * 3, axis=1)
    inside = jnp.concatenate([rows_ref[1]] * 3, axis=1) > 0.5

    def d_theta(a):
        return 0.5 * (pltpu.roll(a, EXT - 1, 0) - pltpu.roll(a, 1, 0))

    def d_phi(a):
        return (pltpu.roll(a, 383, 1) - pltpu.roll(a, 1, 1)) * scale

    def d_rad(pair):
        return [0.5 * pair[1], -0.5 * pair[0]]

    def curl(f):
        rad, colat, lon = f
        lon_r, colat_r = d_rad(lon), d_rad(colat)
        return [
            [d_theta(lon[r]) - d_phi(colat[r]) for r in range(2)],
            [d_phi(rad[r]) - lon_r[r] for r in range(2)],
            [colat_r[r] - d_theta(rad[r]) for r in range(2)],
        ]

    def cross(a, b):
        return [a[1] * b[2] - a[2] * b[1], a[2] * b[0] - a[0] * b[2], a[0] * b[1] - a[1] * b[0]]

    magnetic = None
    for _ in range(STEPS):
        magnetic = [[jnp.where(inside, b, 0.0) for b in pair] for pair in curl(field)]
        current = curl(magnetic)
        for r in range(2):
            b = [magnetic[c][r] for c in range(3)]
            j = [current[c][r] for c in range(3)]
            weight = 1.0 / (b[0] * b[0] + b[1] * b[1] + b[2] * b[2] + soft_floor)
            velocity = [f * weight for f in cross(j, b)]
            push = cross(velocity, b)
            for c in range(3):
                moved = field[c][r] + time_step * (push[c] - resist * j[c])
                field[c][r] = jnp.where(inside, moved, 0.0)

    def centre(a):
        a = pltpu.roll(pltpu.roll(a, EXT - HALO, 0), 384 - HALO, 1)
        return a[0:BAND, 0:SECTOR]

    for c in range(3):
        for r in range(2):
            pot_ref[c, r] = centre(field[c][r])
            mag_ref[c, r] = centre(magnetic[c][r])


def relax(received, table_high, table_low, rows):
    shape = jax.ShapeDtypeStruct((3, 2, BAND, SECTOR), jnp.float32)
    vmem = pl.BlockSpec(memory_space=pltpu.VMEM)
    return pl.pallas_call(
        relax_kernel,
        out_shape=(shape, shape),
        in_specs=[vmem] * 4,
        out_specs=(vmem, vmem),
        scratch_shapes=[
            pltpu.VMEM((1024, 256), jnp.bfloat16),
            pltpu.VMEM((1024, 256), jnp.bfloat16),
            pltpu.VMEM((384, 256), jnp.float32),
            pltpu.VMEM((3, 256, 128), jnp.float32),
        ],
        compiler_params=pltpu.CompilerParams(vmem_limit_bytes=40 * 1024 * 1024),
        name="relaxation",
    )(received, table_high, table_low, rows)


def per_device(coefficients, pair_orders):
    lat_pos = lax.axis_index("lat")
    lon_pos = lax.axis_index("lon")
    own_orders = lax.dynamic_slice_in_dim(pair_orders, lat_pos * PAIRS_LOCAL, PAIRS_LOCAL)
    send = synthesize(own_orders, coefficients).reshape(LAT, 1, CHUNKS * 128)
    received = lax.all_to_all(
        send, "lat", split_axis=0, concat_axis=0, tiled=True, axis_index_groups=[EXCHANGE]
    ).reshape(LAT * CHUNKS, 128)

    by_pair = pair_orders.reshape(LAT, PAIRS_LOCAL)
    by_pair = jnp.concatenate([by_pair[:HALF], by_pair[HALF:][::-1]], axis=0).T
    orders = jnp.stack([by_pair, ORDERS - 1 - by_pair], axis=1)
    orders = jnp.broadcast_to(orders[:, :, None, :], (PAIRS_LOCAL, 2, 2, LAT)).reshape(1, 1024)
    is_cos = (jnp.arange(1024, dtype=jnp.int32)[None, :] // LAT) % 2 == 0
    columns = lon_pos * SECTOR - HALO + jnp.arange(COLS, dtype=jnp.int32)[:, None]
    turns = (orders * columns + jnp.where(is_cos, NP // 4, 0)) & (NP - 1)
    table = jnp.sin(turns.astype(jnp.float32) * (2.0 * math.pi / NP))
    rounded = lax.reduce_precision(table, exponent_bits=8, mantissa_bits=7)
    table_high = rounded.astype(jnp.bfloat16)
    table_low = (table - rounded).astype(jnp.bfloat16)

    row_ids = lat_pos * BAND - HALO + jnp.arange(EXT, dtype=jnp.int32)
    theta = span_start + (row_ids.astype(jnp.float32) + 0.5) * (span_width / NT)
    scale = 1.0 / (2.0 * (3.0 * NT / NP) * jnp.sin(theta))
    inside = ((row_ids >= 0) & (row_ids < NT)).astype(jnp.float32)
    rows = jnp.broadcast_to(jnp.stack([scale, inside])[:, :, None], (2, EXT, 128))
    return relax(received, table_high, table_low, rows)


def solution(mesh):
    in_specs = (P("lat", None, None, None, None), P())
    out_specs = (P(None, None, "lat", "lon"), P(None, None, "lat", "lon"))
    return jax.shard_map(
        per_device, mesh=mesh, in_specs=in_specs, out_specs=out_specs, check_vma=False
    )
```

```python
import math

import jax
import jax.numpy as jnp
import numpy as np
from jax import lax
from jax.experimental import pallas as pl
from jax.experimental.pallas import tpu as pltpu
from jax.sharding import PartitionSpec as P

ORDERS = 512
NT = 1024
NP = 2048
STEPS = 2
LAT = 64
LON = 8
BAND = NT // LAT
SECTOR = NP // LON
HALO = 4
EXT = BAND + 2 * HALO
PAIRS_LOCAL = 4
HALF = LAT // 2
CHUNKS = 9
COLS = SECTOR + 16

soft_floor = 1.0
resist = 0.2
time_step = 0.3
rescale_at = 1.0e10
block_steps = 16
span_start = math.pi / 6.0
span_width = 2.0 * math.pi / 3.0

EXCHANGE = list(range(HALF)) + [LAT - 1 - u for u in range(HALF)]


def own_rows(core):
    first = [2 * core, 2 * core + 1, 4 + 2 * core, 5 + 2 * core]
    return first + [BAND - 1 - r for r in reversed(first)]


def geometry():
    own = np.array([own_rows(0), own_rows(1)])
    rows = BAND * np.arange(HALF)[None, None, :] + own[:, :, None]
    theta = span_start + (rows + 0.5) * (span_width / NT)
    cosine = np.tile(np.cos(theta), (1, 1, PAIRS_LOCAL))
    log_sin = np.tile(np.log(np.sin(theta)), (1, 1, PAIRS_LOCAL))
    return np.stack([cosine, log_sin], axis=1).astype(np.float32)


def norm_logs():
    k = np.arange(1, ORDERS, dtype=np.float64)
    logs = np.concatenate([[0.0], np.cumsum(0.5 * np.log((2 * k + 1) / (2 * k)))])
    return (logs - 0.5 * np.log(4 * np.pi)).astype(np.float32)


def split2(value):
    high = value.astype(jnp.bfloat16)
    low = (value - high.astype(jnp.float32)).astype(jnp.bfloat16)
    return high, low


def dot(a, b):
    return jnp.dot(a, b, preferred_element_type=jnp.float32)


def synth_kernel(
    order_hbm, log_hbm, geom_hbm, coef_hbm, out_ref,
    order_ref, log_ref, geom_ref, coef_ref, fac_ref, back_ref, leg_ref, coefs_ref, wh_ref, wl_ref, stack_ref,
    sems,
):
    lat_pos = lax.axis_index("lat")
    core = lax.axis_index("lon") % 2
    copies = [
        pltpu.make_async_copy(order_hbm, order_ref, sems.at[0]),
        pltpu.make_async_copy(log_hbm, log_ref, sems.at[1]),
        pltpu.make_async_copy(geom_hbm.at[core], geom_ref, sems.at[2]),
        pltpu.make_async_copy(coef_hbm, coef_ref, sems.at[3]),
    ]
    for copy in copies:
        copy.start()
    coefs_ref[...] = jnp.zeros_like(coefs_ref)
    lane = lax.broadcasted_iota(jnp.int32, (8, 128), 1)
    pair_of_lane = lane // HALF

    def per_pair(values):
        result = jnp.full((8, 128), values[0], values[0].dtype)
        for p in range(1, PAIRS_LOCAL):
            result = jnp.where(pair_of_lane == p, values[p], result)
        return result

    copies[0].wait()
    lows = [order_ref[lat_pos * PAIRS_LOCAL + p] for p in range(PAIRS_LOCAL)]
    low = per_pair([o.astype(jnp.float32) for o in lows])
    high = (ORDERS - 1.0) - low
    switch = ORDERS - low

    for c in range(65):
        step = lax.broadcasted_iota(jnp.int32, (8, 128), 0).astype(jnp.float32) + float(8 * c)
        if c < 32:
            order, degree = low, low + step
        else:
            low_side = step < switch
            order = jnp.where(low_side, low, high)
            degree = jnp.where(low_side, low + step, step - 1.0)
        prior = degree - 1.0
        order2 = order * order
        degree2 = degree * degree
        prior2 = prior * prior
        factor = jnp.sqrt(jnp.maximum(4.0 * degree2 - 1.0, 1.0) / jnp.maximum(degree2 - order2, 1.0))
        back = jnp.sqrt(jnp.maximum(prior2 - order2, 0.0) / jnp.maximum(4.0 * prior2 - 1.0, 1.0))
        fac_ref[8 * c:8 * c + 8, :] = factor
        back_ref[8 * c:8 * c + 8, :] = jnp.where(prior > order, factor * back, 0.0)

    copies[1].wait()
    copies[2].wait()
    cosine = geom_ref[0]
    log_sin = geom_ref[1]
    norm_low = per_pair([log_ref[o] for o in lows])
    norm_high = per_pair([log_ref[ORDERS - 1 - o] for o in lows])
    seed_low = norm_low + low * log_sin
    seed_high = norm_high + high * log_sin
    start_scale = jnp.exp(seed_high)
    log_big = math.log(rescale_at)

    def run(base, count, state, restart, first):
        previous, current, scaling, scale = state
        for k in range(count):
            s = base + k
            fac = fac_ref[pl.ds(s, 1), :]
            back = back_ref[pl.ds(s, 1), :]
            if first and k == 0:
                value = jnp.ones((8, 128), jnp.float32)
            else:
                value = (fac * cosine) * current - back * previous
            if restart:
                starting = switch == (s.astype(jnp.float32) if not isinstance(s, int) else float(s))
                value = jnp.where(starting, 1.0, value)
                scaling = jnp.where(starting, seed_high, scaling)
                scale = jnp.where(starting, start_scale, scale)
            previous, current = current, value
            at = s * 8 if isinstance(s, int) else pl.multiple_of(s * 8, 8)
            leg_ref[pl.ds(at, 8), :] = value * scale
        big = jnp.abs(current) > rescale_at
        shrink = jnp.where(big, 1.0 / rescale_at, 1.0)
        scaling = scaling + jnp.where(big, log_big, 0.0)
        return previous * shrink, current * shrink, scaling, jnp.exp(scaling)

    zero = jnp.zeros((8, 128), jnp.float32)
    state = run(0, block_steps, (zero, zero, seed_low, jnp.exp(seed_low)), False, True)
    state = lax.fori_loop(
        1, 16, lambda b, st: run(b * block_steps, block_steps, st, False, False), state
    )
    state = lax.fori_loop(
        16, 32, lambda b, st: run(b * block_steps, block_steps, st, True, False), state
    )
    run(512, 1, state, True, False)

    copies[3].wait()
    for p in range(PAIRS_LOCAL):
        for x in range(2):
            for c in range(3):
                row = (p * 2 + x) * 8 + c * 2
                coefs_ref[row:row + 2, 0:513] = coef_ref[p, x, c]
    slot = lax.broadcasted_iota(jnp.int32, (8, 512), 1)
    for p in range(PAIRS_LOCAL):
        is_low = slot < ORDERS - lows[p]
        low_sign = 1.0 - 2.0 * (slot % 2).astype(jnp.float32)
        high_sign = 1.0 - 2.0 * ((slot + lows[p]) % 2).astype(jnp.float32)
        for x in range(2):
            row = (p * 2 + x) * 8
            both = coefs_ref[row:row + 8, 0:512]
            parts = [jnp.where(is_low, both, 0.0), jnp.where(is_low, 0.0, both)]
            for side in range(2):
                for h in range(2):
                    w = parts[h] if side == 0 else parts[h] * (low_sign if h == 0 else high_sign)
                    at = (((side * PAIRS_LOCAL + p) * 2 + h) * 2 + x) * 8
                    wh, wl = split2(w)
                    wh_ref[at:at + 8, :] = wh.astype(jnp.float32)
                    wl_ref[at:at + 8, :] = wl.astype(jnp.float32)

    tail_sign = per_pair([1.0 - 2.0 * (o % 2).astype(jnp.float32) for o in lows])
    tails = []
    for x in range(2):
        tail = jnp.zeros((8, 128), jnp.float32)
        for p in range(PAIRS_LOCAL):
            row = (p * 2 + x) * 8
            column = jnp.broadcast_to(coefs_ref[row:row + 8, 512:513], (8, 128))
            tail = jnp.where(pair_of_lane == p, column, tail)
        tails.append(tail)
    wh = wh_ref[...].astype(jnp.bfloat16)
    wl = wl_ref[...].astype(jnp.bfloat16)
    for t0 in range(0, 8, 2):
        values = jnp.concatenate(
            [leg_ref[pl.ds(t0 + d, 512, stride=8), :] for d in range(2)], axis=1
        )
        vh, vl = split2(values)
        summed = dot(wh, vh) + dot(wl, vh) + dot(wh, vl)
        for d in range(2):
            t = t0 + d
            last = leg_ref[pl.ds(512 * 8 + t, 1), :]
            part = summed[:, 128 * d:128 * d + 128]
            for side in range(2):
                for h in range(2):
                    for x in range(2):
                        picked = None
                        for p in range(PAIRS_LOCAL):
                            at = (((side * PAIRS_LOCAL + p) * 2 + h) * 2 + x) * 8
                            block = part[at:at + 8, :]
                            picked = block if p == 0 else jnp.where(pair_of_lane == p, block, picked)
                        if h == 1:
                            term = tails[x] * last
                            picked = picked + (term if side == 0 else term * tail_sign)
                        q = 2 + (t if side == 0 else 7 - t)
                        stack_ref[(side * 2 + h) * 2 + x, 6 * q:6 * q + 6, :] = picked[0:6]

    unit = lax.broadcasted_iota(jnp.int32, (12, 128), 1) % HALF
    for h in range(2):
        for x in range(2):
            north, south = h * 2 + x, 4 + h * 2 + x
            n_first, n_last = stack_ref[north, 12:24, :], stack_ref[north, 48:60, :]
            s_first, s_last = stack_ref[south, 12:24, :], stack_ref[south, 48:60, :]
            stack_ref[north, 0:12, :] = jnp.where(unit == 0, 0.0, pltpu.roll(n_last, 1, 1))
            stack_ref[north, 60:72, :] = jnp.where(unit == HALF - 1, s_first, pltpu.roll(n_first, 127, 1))
            stack_ref[south, 0:12, :] = jnp.where(unit == HALF - 1, n_last, pltpu.roll(s_last, 127, 1))
            stack_ref[south, 60:72, :] = jnp.where(unit == 0, 0.0, pltpu.roll(s_first, 1, 1))

    group = lax.broadcasted_iota(jnp.int32, (HALF, 128), 1) // HALF
    for side in range(2):
        for h in range(2):
            which = (side * 2 + h) * 2
            turned = jnp.concatenate([stack_ref[which, 0:64, :], stack_ref[which + 1, 0:64, :]], axis=0).T
            for p in range(PAIRS_LOCAL):
                out_ref[pl.ds(side * HALF * CHUNKS + p * 2 + h, HALF, stride=CHUNKS), :] = turned[
                    HALF * p:HALF * p + HALF, :
                ]
        rest = jnp.concatenate([stack_ref[side * 4 + k, 64:72, :] for k in range(4)] * PAIRS_LOCAL, axis=0).T
        picked = rest[0:HALF, :]
        for p in range(1, PAIRS_LOCAL):
            picked = jnp.where(group == p, rest[HALF * p:HALF * p + HALF, :], picked)
        out_ref[pl.ds(side * HALF * CHUNKS + 8, HALF, stride=CHUNKS), :] = picked


def synthesize(pair_orders, coefficients):
    hbm = pl.BlockSpec(memory_space=pltpu.HBM)
    scratch = [
        pltpu.SMEM((256,), jnp.int32),
        pltpu.SMEM((512,), jnp.float32),
        pltpu.VMEM((2, 8, 128), jnp.float32),
        pltpu.VMEM((4, 2, 3, 2, 513), jnp.float32),
        pltpu.VMEM((520, 128), jnp.float32),
        pltpu.VMEM((520, 128), jnp.float32),
        pltpu.VMEM((520 * 8, 128), jnp.float32),
        pltpu.VMEM((64, 640), jnp.float32),
        pltpu.VMEM((256, 512), jnp.float32),
        pltpu.VMEM((256, 512), jnp.float32),
        pltpu.VMEM((8, 72, 128), jnp.float32),
        pltpu.SemaphoreType.DMA((4,)),
    ]
    return pl.pallas_call(
        synth_kernel,
        out_shape=jax.ShapeDtypeStruct((LAT * CHUNKS, 128), jnp.float32),
        in_specs=[hbm] * 4,
        out_specs=pl.BlockSpec(memory_space=pltpu.VMEM),
        scratch_shapes=scratch,
        compiler_params=pltpu.CompilerParams(vmem_limit_bytes=60 * 1024 * 1024),
        name="synthesis",
    )(pair_orders, norm_logs(), geometry(), coefficients)


def relax_kernel(recv_ref, th_ref, tl_ref, rows_ref, pot_ref, mag_ref, dh_ref, dl_ref, turn_ref, plane_ref):
    lane = lax.broadcasted_iota(jnp.int32, (LAT, 128), 1)
    for half in range(2):
        start = half * LAT * CHUNKS
        at = half * 128
        rest = recv_ref[pl.ds(start + 8, LAT, stride=CHUNKS), :]
        for both in range(8):
            main = recv_ref[pl.ds(start + both, LAT, stride=CHUNKS), :]
            for x in range(2):
                ox = both * 2 + x
                head = pltpu.roll(main, 64, 1) if x else main
                shift = (64 - 8 * ox) % 128
                tail = pltpu.roll(rest, shift, 1) if shift else rest
                high, low = split2(jnp.where(lane < 64, head, tail))
                dh_ref[ox * LAT:ox * LAT + LAT, at:at + 128] = high
                dl_ref[ox * LAT:ox * LAT + LAT, at:at + 128] = low
    dh, dl = dh_ref[...], dl_ref[...]
    th, tl = th_ref[...], tl_ref[...]
    turn_ref[0:COLS, :] = dot(th, dh) + dot(tl, dh) + dot(th, dl)
    turn_ref[COLS:, :] = jnp.zeros((384 - COLS, 256), jnp.float32)
    for j in range(3):
        for half in range(2):
            turned = turn_ref[128 * j:128 * j + 128, 128 * half:128 * half + 128].T
            starts = [2 - 2 * half] + [HALO + r for r in own_rows(half)[::2]] + [20 + 2 * half]
            for k, e in enumerate(starts):
                plane_ref[j, 6 * e:6 * e + 12, :] = turned[12 * k:12 * k + 12, :]
    planes = [
        jnp.concatenate([plane_ref[j, pl.ds(cr, EXT, stride=6), :] for j in range(3)], axis=1)
        for cr in range(6)
    ]
    field = [[planes[c * 2 + r] for r in range(2)] for c in range(3)]
    scale = jnp.concatenate([rows_ref[0]] * 3, axis=1)
    inside = jnp.concatenate([rows_ref[1]] * 3, axis=1) > 0.5

    def d_theta(a):
        return 0.5 * (pltpu.roll(a, EXT - 1, 0) - pltpu.roll(a, 1, 0))

    def d_phi(a):
        return (pltpu.roll(a, 383, 1) - pltpu.roll(a, 1, 1)) * scale

    def d_rad(pair):
        return [0.5 * pair[1], -0.5 * pair[0]]

    def curl(f):
        rad, colat, lon = f
        lon_r, colat_r = d_rad(lon), d_rad(colat)
        return [
            [d_theta(lon[r]) - d_phi(colat[r]) for r in range(2)],
            [d_phi(rad[r]) - lon_r[r] for r in range(2)],
            [colat_r[r] - d_theta(rad[r]) for r in range(2)],
        ]

    def cross(a, b):
        return [a[1] * b[2] - a[2] * b[1], a[2] * b[0] - a[0] * b[2], a[0] * b[1] - a[1] * b[0]]

    magnetic = None
    for _ in range(STEPS):
        magnetic = [[jnp.where(inside, b, 0.0) for b in pair] for pair in curl(field)]
        current = curl(magnetic)
        for r in range(2):
            b = [magnetic[c][r] for c in range(3)]
            j = [current[c][r] for c in range(3)]
            weight = 1.0 / (b[0] * b[0] + b[1] * b[1] + b[2] * b[2] + soft_floor)
            velocity = [f * weight for f in cross(j, b)]
            push = cross(velocity, b)
            for c in range(3):
                moved = field[c][r] + time_step * (push[c] - resist * j[c])
                field[c][r] = jnp.where(inside, moved, 0.0)

    def centre(a):
        a = pltpu.roll(pltpu.roll(a, EXT - HALO, 0), 384 - HALO, 1)
        return a[0:BAND, 0:SECTOR]

    for c in range(3):
        for r in range(2):
            pot_ref[c, r] = centre(field[c][r])
            mag_ref[c, r] = centre(magnetic[c][r])


def relax(received, table_high, table_low, rows):
    shape = jax.ShapeDtypeStruct((3, 2, BAND, SECTOR), jnp.float32)
    vmem = pl.BlockSpec(memory_space=pltpu.VMEM)
    return pl.pallas_call(
        relax_kernel,
        out_shape=(shape, shape),
        in_specs=[vmem] * 4,
        out_specs=(vmem, vmem),
        scratch_shapes=[
            pltpu.VMEM((1024, 256), jnp.bfloat16),
            pltpu.VMEM((1024, 256), jnp.bfloat16),
            pltpu.VMEM((384, 256), jnp.float32),
            pltpu.VMEM((3, 144, 128), jnp.float32),
        ],
        compiler_params=pltpu.CompilerParams(vmem_limit_bytes=40 * 1024 * 1024),
        name="relaxation",
    )(received, table_high, table_low, rows)


def per_device(coefficients, pair_orders):
    lat_pos = lax.axis_index("lat")
    lon_pos = lax.axis_index("lon")
    send = synthesize(pair_orders, coefficients).reshape(LAT, 1, CHUNKS * 128)
    half = lax.all_to_all(
        send, "lat", split_axis=0, concat_axis=0, tiled=True, axis_index_groups=[EXCHANGE]
    ).reshape(LAT * CHUNKS, 128)
    cores = [[2 * i, 2 * i + 1] for i in range(LON // 2)]
    received = lax.all_gather(half, "lon", axis=0, tiled=True, axis_index_groups=cores)

    by_pair = pair_orders.reshape(LAT, PAIRS_LOCAL)
    by_pair = jnp.concatenate([by_pair[:HALF], by_pair[HALF:][::-1]], axis=0).T
    orders = jnp.stack([by_pair, ORDERS - 1 - by_pair], axis=1)
    orders = jnp.broadcast_to(orders[:, :, None, :], (PAIRS_LOCAL, 2, 2, LAT)).reshape(1, 1024)
    is_cos = (jnp.arange(1024, dtype=jnp.int32)[None, :] // LAT) % 2 == 0
    columns = lon_pos * SECTOR - HALO + jnp.arange(COLS, dtype=jnp.int32)[:, None]
    turns = (orders * columns + jnp.where(is_cos, NP // 4, 0)) & (NP - 1)
    table = jnp.sin(turns.astype(jnp.float32) * (2.0 * math.pi / NP))
    rounded = lax.reduce_precision(table, exponent_bits=8, mantissa_bits=7)
    table_high = rounded.astype(jnp.bfloat16)
    table_low = (table - rounded).astype(jnp.bfloat16)

    row_ids = lat_pos * BAND - HALO + jnp.arange(EXT, dtype=jnp.int32)
    theta = span_start + (row_ids.astype(jnp.float32) + 0.5) * (span_width / NT)
    scale = 1.0 / (2.0 * (3.0 * NT / NP) * jnp.sin(theta))
    inside = ((row_ids >= 0) & (row_ids < NT)).astype(jnp.float32)
    rows = jnp.broadcast_to(jnp.stack([scale, inside])[:, :, None], (2, EXT, 128))
    return relax(received, table_high, table_low, rows)


def solution(mesh):
    in_specs = (P("lat", None, None, None, None), P())
    out_specs = (P(None, None, "lat", "lon"), P(None, None, "lat", "lon"))
    return jax.shard_map(
        per_device, mesh=mesh, in_specs=in_specs, out_specs=out_specs, check_vma=False
    )
```

```python
import math

import jax
import jax.numpy as jnp
import numpy as np
from jax import lax
from jax.experimental import pallas as pl
from jax.experimental.pallas import tpu as pltpu
from jax.sharding import PartitionSpec as P

ORDERS = 512
NT = 1024
NP = 2048
STEPS = 2
LAT = 64
LON = 8
BAND = NT // LAT
SECTOR = NP // LON
HALO = 4
EXT = BAND + 2 * HALO
PAIRS_LOCAL = 4
HALF = LAT // 2
CHUNKS = 9
COLS = SECTOR + 16

soft_floor = 1.0
resist = 0.2
time_step = 0.3
rescale_at = 1.0e10
block_steps = 16
span_start = math.pi / 6.0
span_width = 2.0 * math.pi / 3.0

LAT_X, LAT_Z = 4, 8
EXCHANGE = [
    y * HALF + x * LAT_Z + z for y in range(2) for z in reversed(range(LAT_Z)) for x in range(LAT_X)
]


def own_rows(core):
    first = [2 * core, 2 * core + 1, 4 + 2 * core, 5 + 2 * core]
    return first + [BAND - 1 - r for r in reversed(first)]


def geometry():
    own = np.array([own_rows(0), own_rows(1)])
    rows = BAND * np.arange(HALF)[None, None, :] + own[:, :, None]
    theta = span_start + (rows + 0.5) * (span_width / NT)
    cosine = np.tile(np.cos(theta), (1, 1, PAIRS_LOCAL))
    log_sin = np.tile(np.log(np.sin(theta)), (1, 1, PAIRS_LOCAL))
    return np.stack([cosine, log_sin], axis=1).astype(np.float32)


def norm_logs():
    k = np.arange(1, ORDERS, dtype=np.float64)
    logs = np.concatenate([[0.0], np.cumsum(0.5 * np.log((2 * k + 1) / (2 * k)))])
    return (logs - 0.5 * np.log(4 * np.pi)).astype(np.float32)


def split2(value):
    high = value.astype(jnp.bfloat16)
    low = (value - high.astype(jnp.float32)).astype(jnp.bfloat16)
    return high, low


def dot(a, b):
    return jnp.dot(a, b, preferred_element_type=jnp.float32)


def synth_kernel(
    order_hbm, log_hbm, geom_hbm, coef_hbm, out_ref,
    order_ref, log_ref, geom_ref, coef_ref, fac_ref, back_ref, leg_ref, coefs_ref, wh_ref, wl_ref, stack_ref,
    sems,
):
    lat_pos = lax.axis_index("lat")
    core = lax.axis_index("lon") % 2
    copies = [
        pltpu.make_async_copy(order_hbm, order_ref, sems.at[0]),
        pltpu.make_async_copy(log_hbm, log_ref, sems.at[1]),
        pltpu.make_async_copy(geom_hbm.at[core], geom_ref, sems.at[2]),
        pltpu.make_async_copy(coef_hbm, coef_ref, sems.at[3]),
    ]
    for copy in copies:
        copy.start()
    coefs_ref[...] = jnp.zeros_like(coefs_ref)
    lane = lax.broadcasted_iota(jnp.int32, (8, 128), 1)
    pair_of_lane = lane // HALF

    def per_pair(values):
        result = jnp.full((8, 128), values[0], values[0].dtype)
        for p in range(1, PAIRS_LOCAL):
            result = jnp.where(pair_of_lane == p, values[p], result)
        return result

    copies[0].wait()
    lows = [order_ref[lat_pos * PAIRS_LOCAL + p] for p in range(PAIRS_LOCAL)]
    low = per_pair([o.astype(jnp.float32) for o in lows])
    high = (ORDERS - 1.0) - low
    switch = ORDERS - low

    for c in range(65):
        step = lax.broadcasted_iota(jnp.int32, (8, 128), 0).astype(jnp.float32) + float(8 * c)
        if c < 32:
            order, degree = low, low + step
        else:
            low_side = step < switch
            order = jnp.where(low_side, low, high)
            degree = jnp.where(low_side, low + step, step - 1.0)
        prior = degree - 1.0
        order2 = order * order
        degree2 = degree * degree
        prior2 = prior * prior
        factor = jnp.sqrt(jnp.maximum(4.0 * degree2 - 1.0, 1.0) / jnp.maximum(degree2 - order2, 1.0))
        back = jnp.sqrt(jnp.maximum(prior2 - order2, 0.0) / jnp.maximum(4.0 * prior2 - 1.0, 1.0))
        fac_ref[8 * c:8 * c + 8, :] = factor
        back_ref[8 * c:8 * c + 8, :] = jnp.where(prior > order, factor * back, 0.0)

    copies[1].wait()
    copies[2].wait()
    cosine = geom_ref[0]
    log_sin = geom_ref[1]
    norm_low = per_pair([log_ref[o] for o in lows])
    norm_high = per_pair([log_ref[ORDERS - 1 - o] for o in lows])
    seed_low = norm_low + low * log_sin
    seed_high = norm_high + high * log_sin
    start_scale = jnp.exp(seed_high)
    log_big = math.log(rescale_at)

    def run(base, count, state, restart, first):
        previous, current, scaling, scale = state
        for k in range(count):
            s = base + k
            fac = fac_ref[pl.ds(s, 1), :]
            back = back_ref[pl.ds(s, 1), :]
            if first and k == 0:
                value = jnp.ones((8, 128), jnp.float32)
            else:
                value = (fac * cosine) * current - back * previous
            if restart:
                starting = switch == (s.astype(jnp.float32) if not isinstance(s, int) else float(s))
                value = jnp.where(starting, 1.0, value)
                scaling = jnp.where(starting, seed_high, scaling)
                scale = jnp.where(starting, start_scale, scale)
            previous, current = current, value
            at = s * 8 if isinstance(s, int) else pl.multiple_of(s * 8, 8)
            leg_ref[pl.ds(at, 8), :] = value * scale
        big = jnp.abs(current) > rescale_at
        shrink = jnp.where(big, 1.0 / rescale_at, 1.0)
        scaling = scaling + jnp.where(big, log_big, 0.0)
        return previous * shrink, current * shrink, scaling, jnp.exp(scaling)

    zero = jnp.zeros((8, 128), jnp.float32)
    state = run(0, block_steps, (zero, zero, seed_low, jnp.exp(seed_low)), False, True)
    state = lax.fori_loop(
        1, 16, lambda b, st: run(b * block_steps, block_steps, st, False, False), state
    )
    state = lax.fori_loop(
        16, 32, lambda b, st: run(b * block_steps, block_steps, st, True, False), state
    )
    run(512, 1, state, True, False)

    copies[3].wait()
    for p in range(PAIRS_LOCAL):
        for x in range(2):
            for c in range(3):
                row = (p * 2 + x) * 8 + c * 2
                coefs_ref[row:row + 2, 0:513] = coef_ref[p, x, c]
    slot = lax.broadcasted_iota(jnp.int32, (8, 512), 1)
    for p in range(PAIRS_LOCAL):
        is_low = slot < ORDERS - lows[p]
        low_sign = 1.0 - 2.0 * (slot % 2).astype(jnp.float32)
        high_sign = 1.0 - 2.0 * ((slot + lows[p]) % 2).astype(jnp.float32)
        for x in range(2):
            row = (p * 2 + x) * 8
            both = coefs_ref[row:row + 8, 0:512]
            parts = [jnp.where(is_low, both, 0.0), jnp.where(is_low, 0.0, both)]
            for side in range(2):
                for h in range(2):
                    w = parts[h] if side == 0 else parts[h] * (low_sign if h == 0 else high_sign)
                    at = (((side * PAIRS_LOCAL + p) * 2 + h) * 2 + x) * 8
                    wh, wl = split2(w)
                    wh_ref[at:at + 8, :] = wh.astype(jnp.float32)
                    wl_ref[at:at + 8, :] = wl.astype(jnp.float32)

    tail_sign = per_pair([1.0 - 2.0 * (o % 2).astype(jnp.float32) for o in lows])
    tails = []
    for x in range(2):
        tail = jnp.zeros((8, 128), jnp.float32)
        for p in range(PAIRS_LOCAL):
            row = (p * 2 + x) * 8
            column = jnp.broadcast_to(coefs_ref[row:row + 8, 512:513], (8, 128))
            tail = jnp.where(pair_of_lane == p, column, tail)
        tails.append(tail)
    wh = wh_ref[...].astype(jnp.bfloat16)
    wl = wl_ref[...].astype(jnp.bfloat16)
    for t0 in range(0, 8, 2):
        values = jnp.concatenate(
            [leg_ref[pl.ds(t0 + d, 512, stride=8), :] for d in range(2)], axis=1
        )
        vh, vl = split2(values)
        summed = dot(wh, vh) + dot(wl, vh) + dot(wh, vl)
        for d in range(2):
            t = t0 + d
            last = leg_ref[pl.ds(512 * 8 + t, 1), :]
            part = summed[:, 128 * d:128 * d + 128]
            for side in range(2):
                for h in range(2):
                    for x in range(2):
                        picked = None
                        for p in range(PAIRS_LOCAL):
                            at = (((side * PAIRS_LOCAL + p) * 2 + h) * 2 + x) * 8
                            block = part[at:at + 8, :]
                            picked = block if p == 0 else jnp.where(pair_of_lane == p, block, picked)
                        if h == 1:
                            term = tails[x] * last
                            picked = picked + (term if side == 0 else term * tail_sign)
                        q = 2 + (t if side == 0 else 7 - t)
                        stack_ref[(side * 2 + h) * 2 + x, 6 * q:6 * q + 6, :] = picked[0:6]

    unit = lax.broadcasted_iota(jnp.int32, (12, 128), 1) % HALF
    for h in range(2):
        for x in range(2):
            north, south = h * 2 + x, 4 + h * 2 + x
            n_first, n_last = stack_ref[north, 12:24, :], stack_ref[north, 48:60, :]
            s_first, s_last = stack_ref[south, 12:24, :], stack_ref[south, 48:60, :]
            stack_ref[north, 0:12, :] = jnp.where(unit == 0, 0.0, pltpu.roll(n_last, 1, 1))
            stack_ref[north, 60:72, :] = jnp.where(unit == HALF - 1, s_first, pltpu.roll(n_first, 127, 1))
            stack_ref[south, 0:12, :] = jnp.where(unit == HALF - 1, n_last, pltpu.roll(s_last, 127, 1))
            stack_ref[south, 60:72, :] = jnp.where(unit == 0, 0.0, pltpu.roll(s_first, 1, 1))

    group = lax.broadcasted_iota(jnp.int32, (HALF, 128), 1) // HALF
    wide = lax.broadcasted_iota(jnp.int32, (128, 128), 1)
    x, z = wide % LAT_X, (wide // LAT_X) % LAT_Z
    base = wide // HALF * HALF
    source = [base + x * LAT_Z + (LAT_Z - 1 - z), base + (LAT_X - 1 - x) * LAT_Z + z]

    def by_member(value, side):
        return jnp.take_along_axis(value, source[side], axis=1)

    for side in range(2):
        for h in range(2):
            which = (side * 2 + h) * 2
            turned = by_member(
                jnp.concatenate([stack_ref[which, 0:64, :], stack_ref[which + 1, 0:64, :]], axis=0), side
            ).T
            for p in range(PAIRS_LOCAL):
                out_ref[pl.ds(side * HALF * CHUNKS + p * 2 + h, HALF, stride=CHUNKS), :] = turned[
                    HALF * p:HALF * p + HALF, :
                ]
        rest = jnp.concatenate([stack_ref[side * 4 + k, 64:72, :] for k in range(4)] * PAIRS_LOCAL, axis=0)
        rest = by_member(rest, side).T
        picked = rest[0:HALF, :]
        for p in range(1, PAIRS_LOCAL):
            picked = jnp.where(group == p, rest[HALF * p:HALF * p + HALF, :], picked)
        out_ref[pl.ds(side * HALF * CHUNKS + 8, HALF, stride=CHUNKS), :] = picked


def synthesize(pair_orders, coefficients):
    hbm = pl.BlockSpec(memory_space=pltpu.HBM)
    scratch = [
        pltpu.SMEM((256,), jnp.int32),
        pltpu.SMEM((512,), jnp.float32),
        pltpu.VMEM((2, 8, 128), jnp.float32),
        pltpu.VMEM((4, 2, 3, 2, 513), jnp.float32),
        pltpu.VMEM((520, 128), jnp.float32),
        pltpu.VMEM((520, 128), jnp.float32),
        pltpu.VMEM((520 * 8, 128), jnp.float32),
        pltpu.VMEM((64, 640), jnp.float32),
        pltpu.VMEM((256, 512), jnp.float32),
        pltpu.VMEM((256, 512), jnp.float32),
        pltpu.VMEM((8, 72, 128), jnp.float32),
        pltpu.SemaphoreType.DMA((4,)),
    ]
    return pl.pallas_call(
        synth_kernel,
        out_shape=jax.ShapeDtypeStruct((LAT * CHUNKS, 128), jnp.float32),
        in_specs=[hbm] * 4,
        out_specs=pl.BlockSpec(memory_space=pltpu.VMEM),
        scratch_shapes=scratch,
        compiler_params=pltpu.CompilerParams(vmem_limit_bytes=60 * 1024 * 1024),
        name="synthesis",
    )(pair_orders, norm_logs(), geometry(), coefficients)


def relax_kernel(recv_ref, th_ref, tl_ref, rows_ref, pot_ref, mag_ref, dh_ref, dl_ref, turn_ref, plane_ref):
    lane = lax.broadcasted_iota(jnp.int32, (LAT, 128), 1)
    for half in range(2):
        start = half * LAT * CHUNKS
        at = half * 128
        rest = recv_ref[pl.ds(start + 8, LAT, stride=CHUNKS), :]
        for both in range(8):
            main = recv_ref[pl.ds(start + both, LAT, stride=CHUNKS), :]
            for x in range(2):
                ox = both * 2 + x
                head = pltpu.roll(main, 64, 1) if x else main
                shift = (64 - 8 * ox) % 128
                tail = pltpu.roll(rest, shift, 1) if shift else rest
                high, low = split2(jnp.where(lane < 64, head, tail))
                dh_ref[ox * LAT:ox * LAT + LAT, at:at + 128] = high
                dl_ref[ox * LAT:ox * LAT + LAT, at:at + 128] = low
    dh, dl = dh_ref[...], dl_ref[...]
    th, tl = th_ref[...], tl_ref[...]
    turn_ref[0:COLS, :] = dot(th, dh) + dot(tl, dh) + dot(th, dl)
    turn_ref[COLS:, :] = jnp.zeros((384 - COLS, 256), jnp.float32)
    for j in range(3):
        for half in range(2):
            turned = turn_ref[128 * j:128 * j + 128, 128 * half:128 * half + 128].T
            starts = [2 - 2 * half] + [HALO + r for r in own_rows(half)[::2]] + [20 + 2 * half]
            for k, e in enumerate(starts):
                plane_ref[j, 6 * e:6 * e + 12, :] = turned[12 * k:12 * k + 12, :]
    planes = [
        jnp.concatenate([plane_ref[j, pl.ds(cr, EXT, stride=6), :] for j in range(3)], axis=1)
        for cr in range(6)
    ]
    field = [[planes[c * 2 + r] for r in range(2)] for c in range(3)]
    scale = jnp.concatenate([rows_ref[0]] * 3, axis=1)
    inside = jnp.concatenate([rows_ref[1]] * 3, axis=1) > 0.5

    def d_theta(a):
        return 0.5 * (pltpu.roll(a, EXT - 1, 0) - pltpu.roll(a, 1, 0))

    def d_phi(a):
        return (pltpu.roll(a, 383, 1) - pltpu.roll(a, 1, 1)) * scale

    def d_rad(pair):
        return [0.5 * pair[1], -0.5 * pair[0]]

    def curl(f):
        rad, colat, lon = f
        lon_r, colat_r = d_rad(lon), d_rad(colat)
        return [
            [d_theta(lon[r]) - d_phi(colat[r]) for r in range(2)],
            [d_phi(rad[r]) - lon_r[r] for r in range(2)],
            [colat_r[r] - d_theta(rad[r]) for r in range(2)],
        ]

    def cross(a, b):
        return [a[1] * b[2] - a[2] * b[1], a[2] * b[0] - a[0] * b[2], a[0] * b[1] - a[1] * b[0]]

    magnetic = None
    for _ in range(STEPS):
        magnetic = [[jnp.where(inside, b, 0.0) for b in pair] for pair in curl(field)]
        current = curl(magnetic)
        for r in range(2):
            b = [magnetic[c][r] for c in range(3)]
            j = [current[c][r] for c in range(3)]
            weight = 1.0 / (b[0] * b[0] + b[1] * b[1] + b[2] * b[2] + soft_floor)
            velocity = [f * weight for f in cross(j, b)]
            push = cross(velocity, b)
            for c in range(3):
                moved = field[c][r] + time_step * (push[c] - resist * j[c])
                field[c][r] = jnp.where(inside, moved, 0.0)

    def centre(a):
        a = pltpu.roll(pltpu.roll(a, EXT - HALO, 0), 384 - HALO, 1)
        return a[0:BAND, 0:SECTOR]

    for c in range(3):
        for r in range(2):
            pot_ref[c, r] = centre(field[c][r])
            mag_ref[c, r] = centre(magnetic[c][r])


def relax(received, table_high, table_low, rows):
    shape = jax.ShapeDtypeStruct((3, 2, BAND, SECTOR), jnp.float32)
    vmem = pl.BlockSpec(memory_space=pltpu.VMEM)
    return pl.pallas_call(
        relax_kernel,
        out_shape=(shape, shape),
        in_specs=[vmem] * 4,
        out_specs=(vmem, vmem),
        scratch_shapes=[
            pltpu.VMEM((1024, 256), jnp.bfloat16),
            pltpu.VMEM((1024, 256), jnp.bfloat16),
            pltpu.VMEM((384, 256), jnp.float32),
            pltpu.VMEM((3, 144, 128), jnp.float32),
        ],
        compiler_params=pltpu.CompilerParams(vmem_limit_bytes=40 * 1024 * 1024),
        name="relaxation",
    )(received, table_high, table_low, rows)


def per_device(coefficients, pair_orders):
    lat_pos = lax.axis_index("lat")
    lon_pos = lax.axis_index("lon")
    send = synthesize(pair_orders, coefficients).reshape(LAT, 1, CHUNKS * 128)
    half = lax.all_to_all(
        send, "lat", split_axis=0, concat_axis=0, tiled=True, axis_index_groups=[EXCHANGE]
    ).reshape(LAT * CHUNKS, 128)
    cores = [[2 * i, 2 * i + 1] for i in range(LON // 2)]
    received = lax.all_gather(half, "lon", axis=0, tiled=True, axis_index_groups=cores)

    by_pair = pair_orders.reshape(LAT, PAIRS_LOCAL)
    by_pair = by_pair.reshape(2, LAT_X, LAT_Z, PAIRS_LOCAL)[:, :, ::-1].transpose(3, 0, 2, 1)
    by_pair = by_pair.reshape(PAIRS_LOCAL, LAT)
    orders = jnp.stack([by_pair, ORDERS - 1 - by_pair], axis=1)
    orders = jnp.broadcast_to(orders[:, :, None, :], (PAIRS_LOCAL, 2, 2, LAT)).reshape(1, 1024)
    is_cos = (jnp.arange(1024, dtype=jnp.int32)[None, :] // LAT) % 2 == 0
    columns = lon_pos * SECTOR - HALO + jnp.arange(COLS, dtype=jnp.int32)[:, None]
    turns = (orders * columns + jnp.where(is_cos, NP // 4, 0)) & (NP - 1)
    table = jnp.sin(turns.astype(jnp.float32) * (2.0 * math.pi / NP))
    rounded = lax.reduce_precision(table, exponent_bits=8, mantissa_bits=7)
    table_high = rounded.astype(jnp.bfloat16)
    table_low = (table - rounded).astype(jnp.bfloat16)

    row_ids = lat_pos * BAND - HALO + jnp.arange(EXT, dtype=jnp.int32)
    theta = span_start + (row_ids.astype(jnp.float32) + 0.5) * (span_width / NT)
    scale = 1.0 / (2.0 * (3.0 * NT / NP) * jnp.sin(theta))
    inside = ((row_ids >= 0) & (row_ids < NT)).astype(jnp.float32)
    rows = jnp.broadcast_to(jnp.stack([scale, inside])[:, :, None], (2, EXT, 128))
    return relax(received, table_high, table_low, rows)


def solution(mesh):
    in_specs = (P("lat", None, None, None, None), P())
    out_specs = (P(None, None, "lat", "lon"), P(None, None, "lat", "lon"))
    return jax.shard_map(
        per_device, mesh=mesh, in_specs=in_specs, out_specs=out_specs, check_vma=False
    )
```

```python
import math

import jax
import jax.numpy as jnp
import numpy as np
from jax import lax
from jax.experimental import pallas as pl
from jax.experimental.pallas import tpu as pltpu
from jax.sharding import PartitionSpec as P

ORDERS = 512
NT = 1024
NP = 2048
STEPS = 2
LAT = 64
LON = 8
BAND = NT // LAT
SECTOR = NP // LON
HALO = 4
EXT = BAND + 2 * HALO
PAIRS_LOCAL = 4
HALF = LAT // 2
CHUNKS = 9
COLS = SECTOR + 16

soft_floor = 1.0
resist = 0.2
time_step = 0.3
rescale_at = 1.0e10
block_steps = 16
span_start = math.pi / 6.0
span_width = 2.0 * math.pi / 3.0

LAT_X, LAT_Z = 4, 8
EXCHANGE = [
    y * HALF + (k + 2) % LAT_X * LAT_Z + z
    for y in range(2)
    for z in reversed(range(LAT_Z))
    for k in range(LAT_X)
]


def own_rows(core):
    first = [2 * core, 2 * core + 1, 4 + 2 * core, 5 + 2 * core]
    return first + [BAND - 1 - r for r in reversed(first)]


def geometry():
    own = np.array([own_rows(0), own_rows(1)])
    rows = BAND * np.arange(HALF)[None, None, :] + own[:, :, None]
    theta = span_start + (rows + 0.5) * (span_width / NT)
    cosine = np.tile(np.cos(theta), (1, 1, PAIRS_LOCAL))
    log_sin = np.tile(np.log(np.sin(theta)), (1, 1, PAIRS_LOCAL))
    return np.stack([cosine, log_sin], axis=1).astype(np.float32)


def norm_logs():
    k = np.arange(1, ORDERS, dtype=np.float64)
    logs = np.concatenate([[0.0], np.cumsum(0.5 * np.log((2 * k + 1) / (2 * k)))])
    return (logs - 0.5 * np.log(4 * np.pi)).astype(np.float32)


def split2(value):
    high = value.astype(jnp.bfloat16)
    low = (value - high.astype(jnp.float32)).astype(jnp.bfloat16)
    return high, low


def dot(a, b):
    return jnp.dot(a, b, preferred_element_type=jnp.float32)


def synth_kernel(
    order_hbm, log_hbm, geom_hbm, coef_hbm, out_ref,
    order_ref, log_ref, geom_ref, coef_ref, fac_ref, back_ref, leg_ref, coefs_ref, wh_ref, wl_ref, stack_ref,
    early_ref, sems,
):
    lat_pos = lax.axis_index("lat")
    core = lax.axis_index("lon") % 2
    copies = [
        pltpu.make_async_copy(order_hbm, order_ref, sems.at[0]),
        pltpu.make_async_copy(log_hbm, log_ref, sems.at[1]),
        pltpu.make_async_copy(geom_hbm.at[core], geom_ref, sems.at[2]),
        pltpu.make_async_copy(coef_hbm, coef_ref, sems.at[3]),
    ]
    for copy in copies:
        copy.start()
    coefs_ref[...] = jnp.zeros_like(coefs_ref)
    lane = lax.broadcasted_iota(jnp.int32, (8, 128), 1)
    pair_of_lane = lane // HALF

    def per_pair(values):
        result = jnp.full((8, 128), values[0], values[0].dtype)
        for p in range(1, PAIRS_LOCAL):
            result = jnp.where(pair_of_lane == p, values[p], result)
        return result

    copies[0].wait()
    lows = [order_ref[lat_pos * PAIRS_LOCAL + p] for p in range(PAIRS_LOCAL)]
    low = per_pair([o.astype(jnp.float32) for o in lows])
    high = (ORDERS - 1.0) - low
    switch = ORDERS - low

    def factors(c):
        step = lax.broadcasted_iota(jnp.int32, (8, 128), 0).astype(jnp.float32) + float(8 * c)
        if c < 32:
            order, degree = low, low + step
        else:
            low_side = step < switch
            order = jnp.where(low_side, low, high)
            degree = jnp.where(low_side, low + step, step - 1.0)
        prior = degree - 1.0
        order2 = order * order
        degree2 = degree * degree
        prior2 = prior * prior
        factor = jnp.sqrt(jnp.maximum(4.0 * degree2 - 1.0, 1.0) / jnp.maximum(degree2 - order2, 1.0))
        back = jnp.sqrt(jnp.maximum(prior2 - order2, 0.0) / jnp.maximum(4.0 * prior2 - 1.0, 1.0))
        fac_ref[8 * c:8 * c + 8, :] = factor
        back_ref[8 * c:8 * c + 8, :] = jnp.where(prior > order, factor * back, 0.0)

    for c in range(32):
        factors(c)

    copies[1].wait()
    copies[2].wait()
    cosine = geom_ref[0]
    log_sin = geom_ref[1]
    norm_low = per_pair([log_ref[o] for o in lows])
    norm_high = per_pair([log_ref[ORDERS - 1 - o] for o in lows])
    seed_low = norm_low + low * log_sin
    seed_high = norm_high + high * log_sin
    start_scale = jnp.exp(seed_high)
    log_big = math.log(rescale_at)

    def run(base, count, state, restart, first):
        previous, current, scaling, scale = state
        for k in range(count):
            s = base + k
            fac = fac_ref[pl.ds(s, 1), :]
            back = back_ref[pl.ds(s, 1), :]
            if first and k == 0:
                value = jnp.ones((8, 128), jnp.float32)
            else:
                value = (fac * cosine) * current - back * previous
            if restart:
                starting = switch == (s.astype(jnp.float32) if not isinstance(s, int) else float(s))
                value = jnp.where(starting, 1.0, value)
                scaling = jnp.where(starting, seed_high, scaling)
                scale = jnp.where(starting, start_scale, scale)
            previous, current = current, value
            at = s * 8 if isinstance(s, int) else pl.multiple_of(s * 8, 8)
            leg_ref[pl.ds(at, 8), :] = value * scale
        big = jnp.abs(current) > rescale_at
        shrink = jnp.where(big, 1.0 / rescale_at, 1.0)
        scaling = scaling + jnp.where(big, log_big, 0.0)
        return previous * shrink, current * shrink, scaling, jnp.exp(scaling)

    zero = jnp.zeros((8, 128), jnp.float32)
    state = (zero, zero, seed_low, jnp.exp(seed_low))
    for b in range(16):
        state = run(b * block_steps, block_steps, state, False, b == 0)
        factors(32 + 2 * b)
        factors(33 + 2 * b)
    factors(64)
    copies[3].wait()
    for p in range(PAIRS_LOCAL):
        for x in range(2):
            for c in range(3):
                row = (p * 2 + x) * 8 + c * 2
                coefs_ref[row:row + 2, 0:513] = coef_ref[p, x, c]
    slot = lax.broadcasted_iota(jnp.int32, (8, 512), 1)
    for p in range(PAIRS_LOCAL):
        is_low = slot < ORDERS - lows[p]
        low_sign = 1.0 - 2.0 * (slot % 2).astype(jnp.float32)
        high_sign = 1.0 - 2.0 * ((slot + lows[p]) % 2).astype(jnp.float32)
        for x in range(2):
            row = (p * 2 + x) * 8
            both = coefs_ref[row:row + 8, 0:512]
            parts = [jnp.where(is_low, both, 0.0), jnp.where(is_low, 0.0, both)]
            for side in range(2):
                for h in range(2):
                    w = parts[h] if side == 0 else parts[h] * (low_sign if h == 0 else high_sign)
                    at = (((h * 2 + side) * PAIRS_LOCAL + p) * 2 + x) * 8
                    wh, wl = split2(w)
                    wh_ref[at:at + 8, :] = wh.astype(jnp.float32)
                    wl_ref[at:at + 8, :] = wl.astype(jnp.float32)

    tail_sign = per_pair([1.0 - 2.0 * (o % 2).astype(jnp.float32) for o in lows])
    tails = []
    for x in range(2):
        tail = jnp.zeros((8, 128), jnp.float32)
        for p in range(PAIRS_LOCAL):
            row = (p * 2 + x) * 8
            column = jnp.broadcast_to(coefs_ref[row:row + 8, 512:513], (8, 128))
            tail = jnp.where(pair_of_lane == p, column, tail)
        tails.append(tail)

    def contract(t0, half):
        at = 256 * half
        values = jnp.concatenate(
            [leg_ref[pl.ds(8 * at + t0 + d, 256, stride=8), :] for d in range(2)], axis=1
        )
        vh, vl = split2(values)
        rows = 256 if half == 1 else 128
        wh = wh_ref[0:rows, at:at + 256].astype(jnp.bfloat16)
        wl = wl_ref[0:rows, at:at + 256].astype(jnp.bfloat16)
        summed = dot(wh, vh) + dot(wl, vh) + dot(wh, vl)
        for d in range(2):
            t = t0 + d
            part = summed[:, 128 * d:128 * d + 128]
            if half == 1:
                last = leg_ref[pl.ds(512 * 8 + t, 1), :]
            for side in range(2):
                for h in range(2 if half == 1 else 1):
                    for x in range(2):
                        picked = None
                        for p in range(PAIRS_LOCAL):
                            row = (((h * 2 + side) * PAIRS_LOCAL + p) * 2 + x) * 8
                            block = part[row:row + 8, :]
                            picked = block if p == 0 else jnp.where(pair_of_lane == p, block, picked)
                        q = 2 + (t if side == 0 else 7 - t)
                        which = (side * 2 + h) * 2 + x
                        if h == 0:
                            keep = (side * 2 + x) * 8 + t
                            if half == 0:
                                early_ref[keep] = picked
                                continue
                            picked = picked + early_ref[keep]
                        else:
                            term = tails[x] * last
                            picked = picked + (term if side == 0 else term * tail_sign)
                        stack_ref[which, 6 * q:6 * q + 6, :] = picked[0:6]

    for part in range(4):
        for b in range(4):
            state = run((16 + 4 * part + b) * block_steps, block_steps, state, True, False)
        contract(2 * part, 0)
    run(512, 1, state, True, False)
    for part in range(4):
        contract(2 * part, 1)

    unit = lax.broadcasted_iota(jnp.int32, (12, 128), 1) % HALF
    for h in range(2):
        for x in range(2):
            north, south = h * 2 + x, 4 + h * 2 + x
            n_first, n_last = stack_ref[north, 12:24, :], stack_ref[north, 48:60, :]
            s_first, s_last = stack_ref[south, 12:24, :], stack_ref[south, 48:60, :]
            stack_ref[north, 0:12, :] = jnp.where(unit == 0, 0.0, pltpu.roll(n_last, 1, 1))
            stack_ref[north, 60:72, :] = jnp.where(unit == HALF - 1, s_first, pltpu.roll(n_first, 127, 1))
            stack_ref[south, 0:12, :] = jnp.where(unit == HALF - 1, n_last, pltpu.roll(s_last, 127, 1))
            stack_ref[south, 60:72, :] = jnp.where(unit == 0, 0.0, pltpu.roll(s_first, 1, 1))

    group = lax.broadcasted_iota(jnp.int32, (HALF, 128), 1) // HALF
    wide = lax.broadcasted_iota(jnp.int32, (128, 128), 1)
    x, z = (wide + 2) % LAT_X, (wide // LAT_X) % LAT_Z
    base = wide // HALF * HALF
    source = [base + x * LAT_Z + (LAT_Z - 1 - z), base + (LAT_X - 1 - x) * LAT_Z + z]

    def by_member(value, side):
        return jnp.take_along_axis(value, source[side], axis=1)

    for side in range(2):
        for h in range(2):
            which = (side * 2 + h) * 2
            turned = by_member(
                jnp.concatenate([stack_ref[which, 0:64, :], stack_ref[which + 1, 0:64, :]], axis=0), side
            ).T
            for p in range(PAIRS_LOCAL):
                out_ref[pl.ds(side * HALF * CHUNKS + p * 2 + h, HALF, stride=CHUNKS), :] = turned[
                    HALF * p:HALF * p + HALF, :
                ]
        rest = jnp.concatenate([stack_ref[side * 4 + k, 64:72, :] for k in range(4)] * PAIRS_LOCAL, axis=0)
        rest = by_member(rest, side).T
        picked = rest[0:HALF, :]
        for p in range(1, PAIRS_LOCAL):
            picked = jnp.where(group == p, rest[HALF * p:HALF * p + HALF, :], picked)
        out_ref[pl.ds(side * HALF * CHUNKS + 8, HALF, stride=CHUNKS), :] = picked


def synthesize(pair_orders, coefficients):
    hbm = pl.BlockSpec(memory_space=pltpu.HBM)
    scratch = [
        pltpu.SMEM((256,), jnp.int32),
        pltpu.SMEM((512,), jnp.float32),
        pltpu.VMEM((2, 8, 128), jnp.float32),
        pltpu.VMEM((4, 2, 3, 2, 513), jnp.float32),
        pltpu.VMEM((520, 128), jnp.float32),
        pltpu.VMEM((520, 128), jnp.float32),
        pltpu.VMEM((520 * 8, 128), jnp.float32),
        pltpu.VMEM((64, 640), jnp.float32),
        pltpu.VMEM((256, 512), jnp.float32),
        pltpu.VMEM((256, 512), jnp.float32),
        pltpu.VMEM((8, 72, 128), jnp.float32),
        pltpu.VMEM((32, 8, 128), jnp.float32),
        pltpu.SemaphoreType.DMA((4,)),
    ]
    return pl.pallas_call(
        synth_kernel,
        out_shape=jax.ShapeDtypeStruct((LAT * CHUNKS, 128), jnp.float32),
        in_specs=[hbm] * 4,
        out_specs=pl.BlockSpec(memory_space=pltpu.VMEM),
        scratch_shapes=scratch,
        compiler_params=pltpu.CompilerParams(vmem_limit_bytes=60 * 1024 * 1024),
        name="synthesis",
    )(pair_orders, norm_logs(), geometry(), coefficients)


def relax_kernel(recv_ref, th_ref, tl_ref, rows_ref, pot_ref, mag_ref, dh_ref, dl_ref, turn_ref, plane_ref):
    lane = lax.broadcasted_iota(jnp.int32, (LAT, 128), 1)
    for half in range(2):
        start = half * LAT * CHUNKS
        at = half * 128
        rest = recv_ref[pl.ds(start + 8, LAT, stride=CHUNKS), :]
        for both in range(8):
            main = recv_ref[pl.ds(start + both, LAT, stride=CHUNKS), :]
            for x in range(2):
                ox = both * 2 + x
                head = pltpu.roll(main, 64, 1) if x else main
                shift = (64 - 8 * ox) % 128
                tail = pltpu.roll(rest, shift, 1) if shift else rest
                high, low = split2(jnp.where(lane < 64, head, tail))
                dh_ref[ox * LAT:ox * LAT + LAT, at:at + 128] = high
                dl_ref[ox * LAT:ox * LAT + LAT, at:at + 128] = low
    dh, dl = dh_ref[...], dl_ref[...]
    th, tl = th_ref[...], tl_ref[...]
    turn_ref[0:COLS, :] = dot(th, dh) + dot(tl, dh) + dot(th, dl)
    turn_ref[COLS:, :] = jnp.zeros((384 - COLS, 256), jnp.float32)
    for j in range(3):
        for half in range(2):
            turned = turn_ref[128 * j:128 * j + 128, 128 * half:128 * half + 128].T
            starts = [2 - 2 * half] + [HALO + r for r in own_rows(half)[::2]] + [20 + 2 * half]
            for k, e in enumerate(starts):
                plane_ref[j, 6 * e:6 * e + 12, :] = turned[12 * k:12 * k + 12, :]
    planes = [
        jnp.concatenate([plane_ref[j, pl.ds(cr, EXT, stride=6), :] for j in range(3)], axis=1)
        for cr in range(6)
    ]
    field = [[planes[c * 2 + r] for r in range(2)] for c in range(3)]
    scale = jnp.concatenate([rows_ref[0]] * 3, axis=1)
    inside = jnp.concatenate([rows_ref[1]] * 3, axis=1) > 0.5

    def d_theta(a):
        return 0.5 * (pltpu.roll(a, EXT - 1, 0) - pltpu.roll(a, 1, 0))

    def d_phi(a):
        return (pltpu.roll(a, 383, 1) - pltpu.roll(a, 1, 1)) * scale

    def d_rad(pair):
        return [0.5 * pair[1], -0.5 * pair[0]]

    def curl(f):
        rad, colat, lon = f
        lon_r, colat_r = d_rad(lon), d_rad(colat)
        return [
            [d_theta(lon[r]) - d_phi(colat[r]) for r in range(2)],
            [d_phi(rad[r]) - lon_r[r] for r in range(2)],
            [colat_r[r] - d_theta(rad[r]) for r in range(2)],
        ]

    def cross(a, b):
        return [a[1] * b[2] - a[2] * b[1], a[2] * b[0] - a[0] * b[2], a[0] * b[1] - a[1] * b[0]]

    magnetic = None
    for _ in range(STEPS):
        magnetic = [[jnp.where(inside, b, 0.0) for b in pair] for pair in curl(field)]
        current = curl(magnetic)
        for r in range(2):
            b = [magnetic[c][r] for c in range(3)]
            j = [current[c][r] for c in range(3)]
            weight = 1.0 / (b[0] * b[0] + b[1] * b[1] + b[2] * b[2] + soft_floor)
            velocity = [f * weight for f in cross(j, b)]
            push = cross(velocity, b)
            for c in range(3):
                moved = field[c][r] + time_step * (push[c] - resist * j[c])
                field[c][r] = jnp.where(inside, moved, 0.0)

    def centre(a):
        a = pltpu.roll(pltpu.roll(a, EXT - HALO, 0), 384 - HALO, 1)
        return a[0:BAND, 0:SECTOR]

    for c in range(3):
        for r in range(2):
            pot_ref[c, r] = centre(field[c][r])
            mag_ref[c, r] = centre(magnetic[c][r])


def relax(received, table_high, table_low, rows):
    shape = jax.ShapeDtypeStruct((3, 2, BAND, SECTOR), jnp.float32)
    vmem = pl.BlockSpec(memory_space=pltpu.VMEM)
    return pl.pallas_call(
        relax_kernel,
        out_shape=(shape, shape),
        in_specs=[vmem] * 4,
        out_specs=(vmem, vmem),
        scratch_shapes=[
            pltpu.VMEM((1024, 256), jnp.bfloat16),
            pltpu.VMEM((1024, 256), jnp.bfloat16),
            pltpu.VMEM((384, 256), jnp.float32),
            pltpu.VMEM((3, 144, 128), jnp.float32),
        ],
        compiler_params=pltpu.CompilerParams(vmem_limit_bytes=40 * 1024 * 1024),
        name="relaxation",
    )(received, table_high, table_low, rows)


def per_device(coefficients, pair_orders):
    lat_pos = lax.axis_index("lat")
    lon_pos = lax.axis_index("lon")
    send = synthesize(pair_orders, coefficients).reshape(LAT, 1, CHUNKS * 128)
    half = lax.all_to_all(
        send, "lat", split_axis=0, concat_axis=0, tiled=True, axis_index_groups=[EXCHANGE]
    ).reshape(LAT * CHUNKS, 128)
    cores = [[2 * i, 2 * i + 1] for i in range(LON // 2)]
    received = lax.all_gather(half, "lon", axis=0, tiled=True, axis_index_groups=cores)

    by_pair = pair_orders.reshape(LAT, PAIRS_LOCAL)
    by_pair = by_pair.reshape(2, LAT_X, LAT_Z, PAIRS_LOCAL)[:, :, ::-1]
    by_pair = jnp.concatenate([by_pair[:, 2:], by_pair[:, :2]], axis=1).transpose(3, 0, 2, 1)
    by_pair = by_pair.reshape(PAIRS_LOCAL, LAT)
    orders = jnp.stack([by_pair, ORDERS - 1 - by_pair], axis=1)
    orders = jnp.broadcast_to(orders[:, :, None, :], (PAIRS_LOCAL, 2, 2, LAT)).reshape(1, 1024)
    is_cos = (jnp.arange(1024, dtype=jnp.int32)[None, :] // LAT) % 2 == 0
    columns = lon_pos * SECTOR - HALO + jnp.arange(COLS, dtype=jnp.int32)[:, None]
    turns = (orders * columns + jnp.where(is_cos, NP // 4, 0)) & (NP - 1)
    table = jnp.sin(turns.astype(jnp.float32) * (2.0 * math.pi / NP))
    rounded = lax.reduce_precision(table, exponent_bits=8, mantissa_bits=7)
    table_high = rounded.astype(jnp.bfloat16)
    table_low = (table - rounded).astype(jnp.bfloat16)

    row_ids = lat_pos * BAND - HALO + jnp.arange(EXT, dtype=jnp.int32)
    theta = span_start + (row_ids.astype(jnp.float32) + 0.5) * (span_width / NT)
    scale = 1.0 / (2.0 * (3.0 * NT / NP) * jnp.sin(theta))
    inside = ((row_ids >= 0) & (row_ids < NT)).astype(jnp.float32)
    rows = jnp.broadcast_to(jnp.stack([scale, inside])[:, :, None], (2, EXT, 128))
    return relax(received, table_high, table_low, rows)


def solution(mesh):
    in_specs = (P("lat", None, None, None, None), P())
    out_specs = (P(None, None, "lat", "lon"), P(None, None, "lat", "lon"))
    return jax.shard_map(
        per_device, mesh=mesh, in_specs=in_specs, out_specs=out_specs, check_vma=False
    )
```

```python
import math

import jax
import jax.numpy as jnp
import numpy as np
from jax import lax
from jax.experimental import pallas as pl
from jax.experimental.pallas import tpu as pltpu
from jax.sharding import PartitionSpec as P

ORDERS = 512
NT = 1024
NP = 2048
STEPS = 2
LAT = 64
LON = 8
BAND = NT // LAT
SECTOR = NP // LON
HALO = 4
EXT = BAND + 2 * HALO
PAIRS_LOCAL = 4
HALF = LAT // 2
CHUNKS = 9
COLS = SECTOR + 16

soft_floor = 1.0
resist = 0.2
time_step = 0.3
rescale_at = 1.0e10
block_steps = 16
span_start = math.pi / 6.0
span_width = 2.0 * math.pi / 3.0

LAT_X, LAT_Z = 4, 8
EXCHANGE = [
    y * HALF + (k + 2) % LAT_X * LAT_Z + z
    for y in range(2)
    for z in reversed(range(LAT_Z))
    for k in range(LAT_X)
]


def own_rows(core):
    first = [2 * core, 2 * core + 1, 4 + 2 * core, 5 + 2 * core]
    return first + [BAND - 1 - r for r in reversed(first)]


def geometry():
    own = np.array([own_rows(0), own_rows(1)])
    rows = BAND * np.arange(HALF)[None, None, :] + own[:, :, None]
    theta = span_start + (rows + 0.5) * (span_width / NT)
    cosine = np.tile(np.cos(theta), (1, 1, PAIRS_LOCAL))
    log_sin = np.tile(np.log(np.sin(theta)), (1, 1, PAIRS_LOCAL))
    return np.stack([cosine, log_sin], axis=1).astype(np.float32)


def norm_logs():
    k = np.arange(1, ORDERS, dtype=np.float64)
    logs = np.concatenate([[0.0], np.cumsum(0.5 * np.log((2 * k + 1) / (2 * k)))])
    return (logs - 0.5 * np.log(4 * np.pi)).astype(np.float32)


def split2(value):
    high = value.astype(jnp.bfloat16)
    low = (value - high.astype(jnp.float32)).astype(jnp.bfloat16)
    return high, low


def dot(a, b):
    return jnp.dot(a, b, preferred_element_type=jnp.float32)


def synth_kernel(
    order_hbm, log_hbm, geom_hbm, coef_hbm, out_ref,
    order_ref, log_ref, geom_ref, coef_ref, fac_ref, back_ref, leg_ref, coefs_ref, wh_ref, wl_ref, stack_ref,
    early_ref, sems,
):
    lat_pos = lax.axis_index("lat")
    core = lax.axis_index("lon") % 2
    copies = [
        pltpu.make_async_copy(order_hbm, order_ref, sems.at[0]),
        pltpu.make_async_copy(log_hbm, log_ref, sems.at[1]),
        pltpu.make_async_copy(geom_hbm.at[core], geom_ref, sems.at[2]),
        pltpu.make_async_copy(coef_hbm, coef_ref, sems.at[3]),
    ]
    for copy in copies:
        copy.start()
    coefs_ref[...] = jnp.zeros_like(coefs_ref)
    lane = lax.broadcasted_iota(jnp.int32, (8, 128), 1)
    pair_of_lane = lane // HALF

    def per_pair(values):
        result = jnp.full((8, 128), values[0], values[0].dtype)
        for p in range(1, PAIRS_LOCAL):
            result = jnp.where(pair_of_lane == p, values[p], result)
        return result

    copies[0].wait()
    lows = [order_ref[lat_pos * PAIRS_LOCAL + p] for p in range(PAIRS_LOCAL)]
    low = per_pair([o.astype(jnp.float32) for o in lows])
    high = (ORDERS - 1.0) - low
    switch = ORDERS - low

    def factors(c):
        step = lax.broadcasted_iota(jnp.int32, (8, 128), 0).astype(jnp.float32) + float(8 * c)
        if c < 32:
            order, degree = low, low + step
        else:
            low_side = step < switch
            order = jnp.where(low_side, low, high)
            degree = jnp.where(low_side, low + step, step - 1.0)
        prior = degree - 1.0
        order2 = order * order
        degree2 = degree * degree
        prior2 = prior * prior
        factor = jnp.sqrt(jnp.maximum(4.0 * degree2 - 1.0, 1.0) / jnp.maximum(degree2 - order2, 1.0))
        back = jnp.sqrt(jnp.maximum(prior2 - order2, 0.0) / jnp.maximum(4.0 * prior2 - 1.0, 1.0))
        if c >= 32:
            factor = jnp.where(degree > order, factor, 0.0)
        fac_ref[8 * c:8 * c + 8, :] = factor
        back_ref[8 * c:8 * c + 8, :] = jnp.where(prior > order, factor * back, 0.0)

    for c in range(32):
        factors(c)

    copies[1].wait()
    copies[2].wait()
    cosine = geom_ref[0]
    log_sin = geom_ref[1]
    norm_low = per_pair([log_ref[o] for o in lows])
    norm_high = per_pair([log_ref[ORDERS - 1 - o] for o in lows])
    seed_low = norm_low + low * log_sin
    seed_high = norm_high + high * log_sin
    start_scale = jnp.exp(seed_high)
    log_big = math.log(rescale_at)

    def run(base, count, state, restart, first):
        previous, current, scaling, scale = state
        for k in range(count):
            s = base + k
            fac = fac_ref[pl.ds(s, 1), :]
            back = back_ref[pl.ds(s, 1), :]
            from_previous = back * previous
            if restart:
                starting = switch == (s.astype(jnp.float32) if not isinstance(s, int) else float(s))
                scaling = jnp.where(starting, seed_high, scaling)
                scale = jnp.where(starting, start_scale, scale)
                value = (fac * cosine) * current + (jnp.where(starting, 1.0, 0.0) - from_previous)
            elif first and k == 0:
                value = jnp.ones((8, 128), jnp.float32)
            else:
                value = (fac * cosine) * current - from_previous
            previous, current = current, value
            at = s * 8 if isinstance(s, int) else pl.multiple_of(s * 8, 8)
            leg_ref[pl.ds(at, 8), :] = value * scale
        big = jnp.abs(current) > rescale_at
        shrink = jnp.where(big, 1.0 / rescale_at, 1.0)
        scaling = scaling + jnp.where(big, log_big, 0.0)
        return previous * shrink, current * shrink, scaling, jnp.exp(scaling)

    zero = jnp.zeros((8, 128), jnp.float32)
    state = (zero, zero, seed_low, jnp.exp(seed_low))
    for b in range(16):
        state = run(b * block_steps, block_steps, state, False, b == 0)
        factors(32 + 2 * b)
        factors(33 + 2 * b)
    factors(64)
    copies[3].wait()
    for p in range(PAIRS_LOCAL):
        for x in range(2):
            for c in range(3):
                row = (p * 2 + x) * 8 + c * 2
                coefs_ref[row:row + 2, 0:513] = coef_ref[p, x, c]
    slot = lax.broadcasted_iota(jnp.int32, (8, 512), 1)
    for p in range(PAIRS_LOCAL):
        is_low = slot < ORDERS - lows[p]
        low_sign = 1.0 - 2.0 * (slot % 2).astype(jnp.float32)
        high_sign = 1.0 - 2.0 * ((slot + lows[p]) % 2).astype(jnp.float32)
        for x in range(2):
            row = (p * 2 + x) * 8
            both = coefs_ref[row:row + 8, 0:512]
            parts = [jnp.where(is_low, both, 0.0), jnp.where(is_low, 0.0, both)]
            for side in range(2):
                for h in range(2):
                    w = parts[h] if side == 0 else parts[h] * (low_sign if h == 0 else high_sign)
                    at = (((h * 2 + side) * PAIRS_LOCAL + p) * 2 + x) * 8
                    wh, wl = split2(w)
                    wh_ref[at:at + 8, :] = wh.astype(jnp.float32)
                    wl_ref[at:at + 8, :] = wl.astype(jnp.float32)

    tail_sign = per_pair([1.0 - 2.0 * (o % 2).astype(jnp.float32) for o in lows])
    tails = []
    for x in range(2):
        tail = jnp.zeros((8, 128), jnp.float32)
        for p in range(PAIRS_LOCAL):
            row = (p * 2 + x) * 8
            column = jnp.broadcast_to(coefs_ref[row:row + 8, 512:513], (8, 128))
            tail = jnp.where(pair_of_lane == p, column, tail)
        tails.append(tail)

    def contract(t0, half):
        at = 256 * half
        values = jnp.concatenate(
            [leg_ref[pl.ds(8 * at + t0 + d, 256, stride=8), :] for d in range(2)], axis=1
        )
        vh, vl = split2(values)
        rows = 256 if half == 1 else 128
        wh = wh_ref[0:rows, at:at + 256].astype(jnp.bfloat16)
        wl = wl_ref[0:rows, at:at + 256].astype(jnp.bfloat16)
        summed = dot(wh, vh) + dot(wl, vh) + dot(wh, vl)
        for d in range(2):
            t = t0 + d
            part = summed[:, 128 * d:128 * d + 128]
            if half == 1:
                last = leg_ref[pl.ds(512 * 8 + t, 1), :]
            for side in range(2):
                for h in range(2 if half == 1 else 1):
                    for x in range(2):
                        picked = None
                        for p in range(PAIRS_LOCAL):
                            row = (((h * 2 + side) * PAIRS_LOCAL + p) * 2 + x) * 8
                            block = part[row:row + 8, :]
                            picked = block if p == 0 else jnp.where(pair_of_lane == p, block, picked)
                        q = 2 + (t if side == 0 else 7 - t)
                        which = (side * 2 + h) * 2 + x
                        if h == 0:
                            keep = (side * 2 + x) * 8 + t
                            if half == 0:
                                early_ref[keep] = picked
                                continue
                            picked = picked + early_ref[keep]
                        else:
                            term = tails[x] * last
                            picked = picked + (term if side == 0 else term * tail_sign)
                        stack_ref[which, 6 * q:6 * q + 6, :] = picked[0:6]

    for part in range(4):
        for b in range(4):
            state = run((16 + 4 * part + b) * block_steps, block_steps, state, True, False)
        contract(2 * part, 0)
    run(512, 1, state, True, False)
    for part in range(4):
        contract(2 * part, 1)

    unit = lax.broadcasted_iota(jnp.int32, (12, 128), 1) % HALF
    for h in range(2):
        for x in range(2):
            north, south = h * 2 + x, 4 + h * 2 + x
            n_first, n_last = stack_ref[north, 12:24, :], stack_ref[north, 48:60, :]
            s_first, s_last = stack_ref[south, 12:24, :], stack_ref[south, 48:60, :]
            stack_ref[north, 0:12, :] = jnp.where(unit == 0, 0.0, pltpu.roll(n_last, 1, 1))
            stack_ref[north, 60:72, :] = jnp.where(unit == HALF - 1, s_first, pltpu.roll(n_first, 127, 1))
            stack_ref[south, 0:12, :] = jnp.where(unit == HALF - 1, n_last, pltpu.roll(s_last, 127, 1))
            stack_ref[south, 60:72, :] = jnp.where(unit == 0, 0.0, pltpu.roll(s_first, 1, 1))

    group = lax.broadcasted_iota(jnp.int32, (HALF, 128), 1) // HALF
    wide = lax.broadcasted_iota(jnp.int32, (128, 128), 1)
    x, z = (wide + 2) % LAT_X, (wide // LAT_X) % LAT_Z
    base = wide // HALF * HALF
    source = [base + x * LAT_Z + (LAT_Z - 1 - z), base + (LAT_X - 1 - x) * LAT_Z + z]

    def by_member(value, side):
        return jnp.take_along_axis(value, source[side], axis=1)

    for side in range(2):
        for h in range(2):
            which = (side * 2 + h) * 2
            turned = by_member(
                jnp.concatenate([stack_ref[which, 0:64, :], stack_ref[which + 1, 0:64, :]], axis=0), side
            ).T
            for p in range(PAIRS_LOCAL):
                out_ref[pl.ds(side * HALF * CHUNKS + p * 2 + h, HALF, stride=CHUNKS), :] = turned[
                    HALF * p:HALF * p + HALF, :
                ]
        rest = jnp.concatenate([stack_ref[side * 4 + k, 64:72, :] for k in range(4)] * PAIRS_LOCAL, axis=0)
        rest = by_member(rest, side).T
        picked = rest[0:HALF, :]
        for p in range(1, PAIRS_LOCAL):
            picked = jnp.where(group == p, rest[HALF * p:HALF * p + HALF, :], picked)
        out_ref[pl.ds(side * HALF * CHUNKS + 8, HALF, stride=CHUNKS), :] = picked


def synthesize(pair_orders, coefficients):
    hbm = pl.BlockSpec(memory_space=pltpu.HBM)
    scratch = [
        pltpu.SMEM((256,), jnp.int32),
        pltpu.SMEM((512,), jnp.float32),
        pltpu.VMEM((2, 8, 128), jnp.float32),
        pltpu.VMEM((4, 2, 3, 2, 513), jnp.float32),
        pltpu.VMEM((520, 128), jnp.float32),
        pltpu.VMEM((520, 128), jnp.float32),
        pltpu.VMEM((520 * 8, 128), jnp.float32),
        pltpu.VMEM((64, 640), jnp.float32),
        pltpu.VMEM((256, 512), jnp.float32),
        pltpu.VMEM((256, 512), jnp.float32),
        pltpu.VMEM((8, 72, 128), jnp.float32),
        pltpu.VMEM((32, 8, 128), jnp.float32),
        pltpu.SemaphoreType.DMA((4,)),
    ]
    return pl.pallas_call(
        synth_kernel,
        out_shape=jax.ShapeDtypeStruct((LAT * CHUNKS, 128), jnp.float32),
        in_specs=[hbm] * 4,
        out_specs=pl.BlockSpec(memory_space=pltpu.VMEM),
        scratch_shapes=scratch,
        compiler_params=pltpu.CompilerParams(vmem_limit_bytes=60 * 1024 * 1024),
        name="synthesis",
    )(pair_orders, norm_logs(), geometry(), coefficients)


def relax_kernel(
    recv_ref, th_ref, tl_ref, rows_ref, pot_hbm, mag_hbm, dh_ref, dl_ref, turn_ref, plane_ref, pot_ref, mag_ref, sems
):
    lane = lax.broadcasted_iota(jnp.int32, (LAT, 128), 1)
    for half in range(2):
        start = half * LAT * CHUNKS
        at = half * 128
        rest = recv_ref[pl.ds(start + 8, LAT, stride=CHUNKS), :]
        crossed = pltpu.roll(rest, 64, 1)
        for both in range(8):
            main = recv_ref[pl.ds(start + both, LAT, stride=CHUNKS), :]
            for x in range(2):
                ox = both * 2 + x
                side = 1 - x
                tail = rest if (ox >= 8) == (side == 1) else crossed
                tail = jnp.where(lane // 8 == side * 8 + ox % 8, tail, 0.0)
                value = jnp.where(lane < 64, main, tail) if x == 0 else jnp.where(lane < 64, tail, main)
                high, low = split2(value)
                row = (x * 8 + both) * LAT
                dh_ref[row:row + LAT, at:at + 128] = high
                dl_ref[row:row + LAT, at:at + 128] = low
    parts = []
    for x in range(2):
        k = slice(512 * x, 512 * x + 512)
        dh, dl, th, tl = dh_ref[k, :], dl_ref[k, :], th_ref[:, k], tl_ref[:, k]
        parts.append(dot(th, dh) + dot(tl, dh) + dot(th, dl))
    for half in range(2):
        block = slice(128 * half, 128 * half + 128)
        turn_ref[0:COLS, block] = parts[0][:, block] + pltpu.roll(parts[1][:, block], 64, 1)
    turn_ref[COLS:, :] = jnp.zeros((384 - COLS, 256), jnp.float32)
    for j in range(3):
        for half in range(2):
            turned = turn_ref[128 * j:128 * j + 128, 128 * half:128 * half + 128].T
            tail = turned[64:72, :]
            for g in range(1, 8):
                tail = tail + turned[64 + 8 * g:72 + 8 * g, :]
            turned = jnp.concatenate([turned[0:64, :], tail], axis=0)
            starts = [2 - 2 * half] + [HALO + r for r in own_rows(half)[::2]] + [20 + 2 * half]
            for k, e in enumerate(starts):
                plane_ref[j, 6 * e:6 * e + 12, :] = turned[12 * k:12 * k + 12, :]
    planes = [
        jnp.concatenate([plane_ref[j, pl.ds(cr, EXT, stride=6), :] for j in range(3)], axis=1)
        for cr in range(6)
    ]
    field = [[planes[c * 2 + r] for r in range(2)] for c in range(3)]
    scale = jnp.concatenate([rows_ref[0]] * 3, axis=1)
    inside = jnp.concatenate([rows_ref[1]] * 3, axis=1) > 0.5

    def d_theta(a):
        return 0.5 * (pltpu.roll(a, EXT - 1, 0) - pltpu.roll(a, 1, 0))

    def d_phi(a):
        return (pltpu.roll(a, 383, 1) - pltpu.roll(a, 1, 1)) * scale

    def d_rad(pair):
        return [0.5 * pair[1], -0.5 * pair[0]]

    def curl(f):
        rad, colat, lon = f
        lon_r, colat_r = d_rad(lon), d_rad(colat)
        return [
            [d_theta(lon[r]) - d_phi(colat[r]) for r in range(2)],
            [d_phi(rad[r]) - lon_r[r] for r in range(2)],
            [colat_r[r] - d_theta(rad[r]) for r in range(2)],
        ]

    def cross(a, b):
        return [a[1] * b[2] - a[2] * b[1], a[2] * b[0] - a[0] * b[2], a[0] * b[1] - a[1] * b[0]]

    def centre(a):
        a = pltpu.roll(pltpu.roll(a, EXT - HALO, 0), 384 - HALO, 1)
        return a[0:BAND, 0:SECTOR]

    pot_copy = pltpu.make_async_copy(pot_ref, pot_hbm, sems.at[0])
    mag_copy = pltpu.make_async_copy(mag_ref, mag_hbm, sems.at[1])
    for step in range(STEPS):
        magnetic = [[jnp.where(inside, b, 0.0) for b in pair] for pair in curl(field)]
        if step == STEPS - 1:
            for c in range(3):
                for r in range(2):
                    mag_ref[c, r] = centre(magnetic[c][r])
            mag_copy.start()
        current = curl(magnetic)
        for r in range(2):
            b = [magnetic[c][r] for c in range(3)]
            j = [current[c][r] for c in range(3)]
            weight = 1.0 / (b[0] * b[0] + b[1] * b[1] + b[2] * b[2] + soft_floor)
            velocity = [f * weight for f in cross(j, b)]
            push = cross(velocity, b)
            for c in range(3):
                moved = field[c][r] + time_step * (push[c] - resist * j[c])
                field[c][r] = jnp.where(inside, moved, 0.0)
    for c in range(3):
        for r in range(2):
            pot_ref[c, r] = centre(field[c][r])
    pot_copy.start()
    mag_copy.wait()
    pot_copy.wait()


def relax(received, table_high, table_low, rows):
    shape = jax.ShapeDtypeStruct((3, 2, BAND, SECTOR), jnp.float32)
    vmem = pl.BlockSpec(memory_space=pltpu.VMEM)
    hbm = pl.BlockSpec(memory_space=pltpu.HBM)
    return pl.pallas_call(
        relax_kernel,
        out_shape=(shape, shape),
        in_specs=[vmem] * 4,
        out_specs=(hbm, hbm),
        scratch_shapes=[
            pltpu.VMEM((1024, 256), jnp.bfloat16),
            pltpu.VMEM((1024, 256), jnp.bfloat16),
            pltpu.VMEM((384, 256), jnp.float32),
            pltpu.VMEM((3, 144, 128), jnp.float32),
            pltpu.VMEM((3, 2, BAND, SECTOR), jnp.float32),
            pltpu.VMEM((3, 2, BAND, SECTOR), jnp.float32),
            pltpu.SemaphoreType.DMA((2,)),
        ],
        compiler_params=pltpu.CompilerParams(vmem_limit_bytes=40 * 1024 * 1024),
        name="relaxation",
    )(received, table_high, table_low, rows)


def per_device(coefficients, pair_orders):
    lat_pos = lax.axis_index("lat")
    lon_pos = lax.axis_index("lon")
    send = synthesize(pair_orders, coefficients).reshape(LAT, 1, CHUNKS * 128)
    half = lax.all_to_all(
        send, "lat", split_axis=0, concat_axis=0, tiled=True, axis_index_groups=[EXCHANGE]
    ).reshape(LAT * CHUNKS, 128)
    cores = [[2 * i, 2 * i + 1] for i in range(LON // 2)]
    received = lax.all_gather(half, "lon", axis=0, tiled=True, axis_index_groups=cores)

    by_pair = pair_orders.reshape(LAT, PAIRS_LOCAL)
    by_pair = by_pair.reshape(2, LAT_X, LAT_Z, PAIRS_LOCAL)[:, :, ::-1]
    by_pair = jnp.concatenate([by_pair[:, 2:], by_pair[:, :2]], axis=1).transpose(3, 0, 2, 1)
    by_pair = by_pair.reshape(PAIRS_LOCAL, LAT)
    orders = jnp.stack([by_pair, ORDERS - 1 - by_pair], axis=1).reshape(1, 512)
    orders = jnp.concatenate([orders, orders], axis=1)
    is_cos = jnp.arange(1024, dtype=jnp.int32)[None, :] < 512
    columns = lon_pos * SECTOR - HALO + jnp.arange(COLS, dtype=jnp.int32)[:, None]
    turns = (orders * columns + jnp.where(is_cos, NP // 4, 0)) & (NP - 1)
    table = jnp.sin(turns.astype(jnp.float32) * (2.0 * math.pi / NP))
    rounded = lax.reduce_precision(table, exponent_bits=8, mantissa_bits=7)
    table_high = rounded.astype(jnp.bfloat16)
    table_low = (table - rounded).astype(jnp.bfloat16)

    row_ids = lat_pos * BAND - HALO + jnp.arange(EXT, dtype=jnp.int32)
    theta = span_start + (row_ids.astype(jnp.float32) + 0.5) * (span_width / NT)
    scale = 1.0 / (2.0 * (3.0 * NT / NP) * jnp.sin(theta))
    inside = ((row_ids >= 0) & (row_ids < NT)).astype(jnp.float32)
    rows = jnp.broadcast_to(jnp.stack([scale, inside])[:, :, None], (2, EXT, 128))
    return relax(received, table_high, table_low, rows)


def solution(mesh):
    in_specs = (P("lat", None, None, None, None), P())
    out_specs = (P(None, None, "lat", "lon"), P(None, None, "lat", "lon"))
    return jax.shard_map(
        per_device, mesh=mesh, in_specs=in_specs, out_specs=out_specs, check_vma=False
    )
```

```python
import math

import jax
import jax.numpy as jnp
import numpy as np
from jax import lax
from jax.experimental import pallas as pl
from jax.experimental.pallas import tpu as pltpu
from jax.sharding import PartitionSpec as P

ORDERS = 512
NT = 1024
NP = 2048
STEPS = 2
LAT = 64
LON = 8
BAND = NT // LAT
SECTOR = NP // LON
HALO = 4
EXT = BAND + 2 * HALO
PAIRS_LOCAL = 4
HALF = LAT // 2
CHUNKS = 9
COLS = SECTOR + 16

soft_floor = 1.0
resist = 0.2
time_step = 0.3
rescale_at = 1.0e10
block_steps = 16
span_start = math.pi / 6.0
span_width = 2.0 * math.pi / 3.0

LAT_X, LAT_Z = 4, 8
EXCHANGE = [
    y * HALF + (k + 2) % LAT_X * LAT_Z + z
    for y in range(2)
    for z in reversed(range(LAT_Z))
    for k in range(LAT_X)
]


def own_rows(core):
    first = [2 * core, 2 * core + 1, 4 + 2 * core, 5 + 2 * core]
    return first + [BAND - 1 - r for r in reversed(first)]


def geometry():
    own = np.array([own_rows(0), own_rows(1)])
    rows = BAND * np.arange(HALF)[None, None, :] + own[:, :, None]
    theta = span_start + (rows + 0.5) * (span_width / NT)
    cosine = np.tile(np.cos(theta), (1, 1, PAIRS_LOCAL))
    log_sin = np.tile(np.log(np.sin(theta)), (1, 1, PAIRS_LOCAL))
    return np.stack([cosine, log_sin], axis=1).astype(np.float32)


def norm_logs():
    k = np.arange(1, ORDERS, dtype=np.float64)
    logs = np.concatenate([[0.0], np.cumsum(0.5 * np.log((2 * k + 1) / (2 * k)))])
    return (logs - 0.5 * np.log(4 * np.pi)).astype(np.float32)


def split2(value):
    high = value.astype(jnp.bfloat16)
    low = (value - high.astype(jnp.float32)).astype(jnp.bfloat16)
    return high, low


def dot(a, b):
    return jnp.dot(a, b, preferred_element_type=jnp.float32)


def synth_kernel(
    order_hbm, log_hbm, geom_hbm, coef_hbm, out_ref,
    order_ref, log_ref, geom_ref, coef_ref, fac_ref, back_ref, leg_ref, coefs_ref, wh_ref, wl_ref, stack_ref,
    early_ref, sems,
):
    lat_pos = lax.axis_index("lat")
    core = lax.axis_index("lon") % 2
    copies = [
        pltpu.make_async_copy(order_hbm, order_ref, sems.at[0]),
        pltpu.make_async_copy(log_hbm, log_ref, sems.at[1]),
        pltpu.make_async_copy(geom_hbm.at[core], geom_ref, sems.at[2]),
        pltpu.make_async_copy(coef_hbm, coef_ref, sems.at[3]),
    ]
    for copy in copies:
        copy.start()
    coefs_ref[...] = jnp.zeros_like(coefs_ref)
    lane = lax.broadcasted_iota(jnp.int32, (8, 128), 1)
    pair_of_lane = lane // HALF

    def per_pair(values):
        result = jnp.full((8, 128), values[0], values[0].dtype)
        for p in range(1, PAIRS_LOCAL):
            result = jnp.where(pair_of_lane == p, values[p], result)
        return result

    copies[0].wait()
    lows = [order_ref[lat_pos * PAIRS_LOCAL + p] for p in range(PAIRS_LOCAL)]
    low = per_pair([o.astype(jnp.float32) for o in lows])
    high = (ORDERS - 1.0) - low
    switch = ORDERS - low

    def factors(c):
        step = lax.broadcasted_iota(jnp.int32, (8, 128), 0).astype(jnp.float32) + float(8 * c)
        if c < 32:
            order, degree = low, low + step
        else:
            low_side = step < switch
            order = jnp.where(low_side, low, high)
            degree = jnp.where(low_side, low + step, step - 1.0)
        prior = degree - 1.0
        order2 = order * order
        degree2 = degree * degree
        prior2 = prior * prior
        factor = jnp.sqrt(jnp.maximum(4.0 * degree2 - 1.0, 1.0) / jnp.maximum(degree2 - order2, 1.0))
        back = jnp.sqrt(jnp.maximum(prior2 - order2, 0.0) / jnp.maximum(4.0 * prior2 - 1.0, 1.0))
        if c >= 32:
            factor = jnp.where(degree > order, factor, 0.0)
        fac_ref[8 * c:8 * c + 8, :] = factor
        back_ref[8 * c:8 * c + 8, :] = jnp.where(prior > order, factor * back, 0.0)

    for c in range(32):
        factors(c)

    copies[1].wait()
    copies[2].wait()
    cosine = geom_ref[0]
    log_sin = geom_ref[1]
    norm_low = per_pair([log_ref[o] for o in lows])
    norm_high = per_pair([log_ref[ORDERS - 1 - o] for o in lows])
    seed_low = norm_low + low * log_sin
    seed_high = norm_high + high * log_sin
    start_scale = jnp.exp(seed_high)
    log_big = math.log(rescale_at)

    def run(base, count, state, restart, first):
        previous, current, scaling, scale = state
        for k in range(count):
            s = base + k
            fac = fac_ref[pl.ds(s, 1), :]
            back = back_ref[pl.ds(s, 1), :]
            from_previous = back * previous
            if restart:
                starting = switch == (s.astype(jnp.float32) if not isinstance(s, int) else float(s))
                scaling = jnp.where(starting, seed_high, scaling)
                scale = jnp.where(starting, start_scale, scale)
                value = (fac * cosine) * current + (jnp.where(starting, 1.0, 0.0) - from_previous)
            elif first and k == 0:
                value = jnp.ones((8, 128), jnp.float32)
            else:
                value = (fac * cosine) * current - from_previous
            previous, current = current, value
            at = s * 8 if isinstance(s, int) else pl.multiple_of(s * 8, 8)
            leg_ref[pl.ds(at, 8), :] = value * scale
        big = jnp.abs(current) > rescale_at
        shrink = jnp.where(big, 1.0 / rescale_at, 1.0)
        scaling = scaling + jnp.where(big, log_big, 0.0)
        return previous * shrink, current * shrink, scaling, jnp.exp(scaling)

    zero = jnp.zeros((8, 128), jnp.float32)
    state = (zero, zero, seed_low, jnp.exp(seed_low))
    for b in range(16):
        state = run(b * block_steps, block_steps, state, False, b == 0)
        factors(32 + 2 * b)
        factors(33 + 2 * b)
    factors(64)
    copies[3].wait()
    for p in range(PAIRS_LOCAL):
        for x in range(2):
            for c in range(3):
                row = (p * 2 + x) * 8 + c * 2
                coefs_ref[row:row + 2, 0:513] = coef_ref[p, x, c]
    slot = lax.broadcasted_iota(jnp.int32, (8, 512), 1)
    for p in range(PAIRS_LOCAL):
        is_low = slot < ORDERS - lows[p]
        low_sign = 1.0 - 2.0 * (slot % 2).astype(jnp.float32)
        high_sign = 1.0 - 2.0 * ((slot + lows[p]) % 2).astype(jnp.float32)
        for x in range(2):
            row = (p * 2 + x) * 8
            both = coefs_ref[row:row + 8, 0:512]
            parts = [jnp.where(is_low, both, 0.0), jnp.where(is_low, 0.0, both)]
            for side in range(2):
                for h in range(2):
                    w = parts[h] if side == 0 else parts[h] * (low_sign if h == 0 else high_sign)
                    at = (((h * 2 + side) * PAIRS_LOCAL + p) * 2 + x) * 8
                    wh, wl = split2(w)
                    wh_ref[at:at + 8, :] = wh.astype(jnp.float32)
                    wl_ref[at:at + 8, :] = wl.astype(jnp.float32)

    tail_sign = per_pair([1.0 - 2.0 * (o % 2).astype(jnp.float32) for o in lows])
    tails = []
    for x in range(2):
        tail = jnp.zeros((8, 128), jnp.float32)
        for p in range(PAIRS_LOCAL):
            row = (p * 2 + x) * 8
            column = jnp.broadcast_to(coefs_ref[row:row + 8, 512:513], (8, 128))
            tail = jnp.where(pair_of_lane == p, column, tail)
        tails.append(tail)

    def contract(t0, half):
        at = 256 * half
        values = jnp.concatenate(
            [leg_ref[pl.ds(8 * at + t0 + d, 256, stride=8), :] for d in range(2)], axis=1
        )
        vh, vl = split2(values)
        rows = 256 if half == 1 else 128
        wh = wh_ref[0:rows, at:at + 256].astype(jnp.bfloat16)
        wl = wl_ref[0:rows, at:at + 256].astype(jnp.bfloat16)
        summed = dot(wh, vh) + dot(wl, vh) + dot(wh, vl)
        for d in range(2):
            t = t0 + d
            part = summed[:, 128 * d:128 * d + 128]
            if half == 1:
                last = leg_ref[pl.ds(512 * 8 + t, 1), :]
            for side in range(2):
                for h in range(2 if half == 1 else 1):
                    for x in range(2):
                        picked = None
                        for p in range(PAIRS_LOCAL):
                            row = (((h * 2 + side) * PAIRS_LOCAL + p) * 2 + x) * 8
                            block = part[row:row + 8, :]
                            picked = block if p == 0 else jnp.where(pair_of_lane == p, block, picked)
                        q = 2 + (t if side == 0 else 7 - t)
                        which = (side * 2 + h) * 2 + x
                        if h == 0:
                            keep = (side * 2 + x) * 8 + t
                            if half == 0:
                                early_ref[keep] = picked
                                continue
                            picked = picked + early_ref[keep]
                        else:
                            term = tails[x] * last
                            picked = picked + (term if side == 0 else term * tail_sign)
                        stack_ref[which, 6 * q:6 * q + 6, :] = picked[0:6]

    for part in range(4):
        for b in range(4):
            state = run((16 + 4 * part + b) * block_steps, block_steps, state, True, False)
        contract(2 * part, 0)
    run(512, 1, state, True, False)
    for part in range(4):
        contract(2 * part, 1)

    unit = lax.broadcasted_iota(jnp.int32, (12, 128), 1) % HALF
    for h in range(2):
        for x in range(2):
            north, south = h * 2 + x, 4 + h * 2 + x
            n_first, n_last = stack_ref[north, 12:24, :], stack_ref[north, 48:60, :]
            s_first, s_last = stack_ref[south, 12:24, :], stack_ref[south, 48:60, :]
            stack_ref[north, 0:12, :] = jnp.where(unit == 0, 0.0, pltpu.roll(n_last, 1, 1))
            stack_ref[north, 60:72, :] = jnp.where(unit == HALF - 1, s_first, pltpu.roll(n_first, 127, 1))
            stack_ref[south, 0:12, :] = jnp.where(unit == HALF - 1, n_last, pltpu.roll(s_last, 127, 1))
            stack_ref[south, 60:72, :] = jnp.where(unit == 0, 0.0, pltpu.roll(s_first, 1, 1))

    group = lax.broadcasted_iota(jnp.int32, (HALF, 128), 1) // HALF
    wide = lax.broadcasted_iota(jnp.int32, (128, 128), 1)
    x, z = (wide + 2) % LAT_X, (wide // LAT_X) % LAT_Z
    base = wide // HALF * HALF
    source = [base + x * LAT_Z + (LAT_Z - 1 - z), base + (LAT_X - 1 - x) * LAT_Z + z]

    def by_member(value, side):
        return jnp.take_along_axis(value, source[side], axis=1)

    for side in range(2):
        for h in range(2):
            which = (side * 2 + h) * 2
            turned = by_member(
                jnp.concatenate([stack_ref[which, 0:64, :], stack_ref[which + 1, 0:64, :]], axis=0), side
            ).T
            for p in range(PAIRS_LOCAL):
                out_ref[pl.ds(side * HALF * CHUNKS + p * 2 + h, HALF, stride=CHUNKS), :] = turned[
                    HALF * p:HALF * p + HALF, :
                ]
        rest = jnp.concatenate([stack_ref[side * 4 + k, 64:72, :] for k in range(4)] * PAIRS_LOCAL, axis=0)
        rest = by_member(rest, side).T
        picked = rest[0:HALF, :]
        for p in range(1, PAIRS_LOCAL):
            picked = jnp.where(group == p, rest[HALF * p:HALF * p + HALF, :], picked)
        out_ref[pl.ds(side * HALF * CHUNKS + 8, HALF, stride=CHUNKS), :] = picked


def synthesize(pair_orders, coefficients):
    hbm = pl.BlockSpec(memory_space=pltpu.HBM)
    scratch = [
        pltpu.SMEM((256,), jnp.int32),
        pltpu.SMEM((512,), jnp.float32),
        pltpu.VMEM((2, 8, 128), jnp.float32),
        pltpu.VMEM((4, 2, 3, 2, 513), jnp.float32),
        pltpu.VMEM((520, 128), jnp.float32),
        pltpu.VMEM((520, 128), jnp.float32),
        pltpu.VMEM((520 * 8, 128), jnp.float32),
        pltpu.VMEM((64, 640), jnp.float32),
        pltpu.VMEM((256, 512), jnp.float32),
        pltpu.VMEM((256, 512), jnp.float32),
        pltpu.VMEM((8, 72, 128), jnp.float32),
        pltpu.VMEM((32, 8, 128), jnp.float32),
        pltpu.SemaphoreType.DMA((4,)),
    ]
    return pl.pallas_call(
        synth_kernel,
        out_shape=jax.ShapeDtypeStruct((LAT * CHUNKS, 128), jnp.float32),
        in_specs=[hbm] * 4,
        out_specs=pl.BlockSpec(memory_space=pltpu.VMEM),
        scratch_shapes=scratch,
        compiler_params=pltpu.CompilerParams(vmem_limit_bytes=60 * 1024 * 1024),
        name="synthesis",
    )(pair_orders, norm_logs(), geometry(), coefficients)


def relax_kernel(
    recv_ref, th_ref, tl_ref, rows_ref, pot_hbm, mag_hbm, dh_ref, dl_ref, turn_ref, plane_ref, pot_ref, mag_ref, sems
):
    lane = lax.broadcasted_iota(jnp.int32, (LAT, 128), 1)
    for half in range(2):
        start = half * LAT * CHUNKS
        at = half * 128
        rest = recv_ref[pl.ds(start + 8, LAT, stride=CHUNKS), :]
        crossed = pltpu.roll(rest, 64, 1)
        for both in range(8):
            main = recv_ref[pl.ds(start + both, LAT, stride=CHUNKS), :]
            for x in range(2):
                ox = both * 2 + x
                side = 1 - x
                tail = rest if (ox >= 8) == (side == 1) else crossed
                tail = jnp.where(lane // 8 == side * 8 + ox % 8, tail, 0.0)
                value = jnp.where(lane < 64, main, tail) if x == 0 else jnp.where(lane < 64, tail, main)
                high, low = split2(value)
                row = (x * 8 + both) * LAT
                dh_ref[row:row + LAT, at:at + 128] = high
                dl_ref[row:row + LAT, at:at + 128] = low
    parts = []
    for x in range(2):
        k = slice(512 * x, 512 * x + 512)
        dh, dl, th, tl = dh_ref[k, :], dl_ref[k, :], th_ref[:, k], tl_ref[:, k]
        parts.append(dot(th, dh) + dot(tl, dh) + dot(th, dl))
    for half in range(2):
        block = slice(128 * half, 128 * half + 128)
        summed = parts[0][:, block] + pltpu.roll(parts[1][:, block], 64, 1)
        turn_ref[0:COLS - 8, block] = summed[0:COLS - 8]
        turn_ref[376:384, block] = summed[COLS - 8:COLS]
    turn_ref[COLS - 8:376, :] = jnp.zeros((384 - COLS, 256), jnp.float32)
    for j in range(3):
        for half in range(2):
            turned = turn_ref[128 * j:128 * j + 128, 128 * half:128 * half + 128].T
            tail = turned[64:72, :]
            for g in range(1, 8):
                tail = tail + turned[64 + 8 * g:72 + 8 * g, :]
            turned = jnp.concatenate([turned[0:64, :], tail], axis=0)
            starts = [2 - 2 * half] + [HALO + r for r in own_rows(half)[::2]] + [20 + 2 * half]
            for k, e in enumerate(starts):
                plane_ref[j, 6 * e:6 * e + 12, :] = turned[12 * k:12 * k + 12, :]
    planes = [
        jnp.concatenate([plane_ref[j, pl.ds(cr, EXT, stride=6), :] for j in range(3)], axis=1)
        for cr in range(6)
    ]
    field = [[planes[c * 2 + r] for r in range(2)] for c in range(3)]
    scale = jnp.concatenate([rows_ref[0]] * 3, axis=1)
    inside = jnp.concatenate([rows_ref[1]] * 3, axis=1) > 0.5

    def d_theta(a):
        return 0.5 * (pltpu.roll(a, EXT - 1, 0) - pltpu.roll(a, 1, 0))

    def d_phi(a):
        return (pltpu.roll(a, 383, 1) - pltpu.roll(a, 1, 1)) * scale

    def d_rad(pair):
        return [0.5 * pair[1], -0.5 * pair[0]]

    def curl(f):
        rad, colat, lon = f
        lon_r, colat_r = d_rad(lon), d_rad(colat)
        return [
            [d_theta(lon[r]) - d_phi(colat[r]) for r in range(2)],
            [d_phi(rad[r]) - lon_r[r] for r in range(2)],
            [colat_r[r] - d_theta(rad[r]) for r in range(2)],
        ]

    def cross(a, b):
        return [a[1] * b[2] - a[2] * b[1], a[2] * b[0] - a[0] * b[2], a[0] * b[1] - a[1] * b[0]]

    def centre(a):
        return pltpu.roll(a[:, 0:SECTOR], EXT - HALO, 0)[0:BAND]

    pot_copy = pltpu.make_async_copy(pot_ref, pot_hbm, sems.at[0])
    mag_copy = pltpu.make_async_copy(mag_ref, mag_hbm, sems.at[1])
    for step in range(STEPS):
        magnetic = [[jnp.where(inside, b, 0.0) for b in pair] for pair in curl(field)]
        if step == STEPS - 1:
            for c in range(3):
                for r in range(2):
                    mag_ref[c, r] = centre(magnetic[c][r])
            mag_copy.start()
        current = curl(magnetic)
        for r in range(2):
            b = [magnetic[c][r] for c in range(3)]
            j = [current[c][r] for c in range(3)]
            weight = 1.0 / (b[0] * b[0] + b[1] * b[1] + b[2] * b[2] + soft_floor)
            velocity = [f * weight for f in cross(j, b)]
            push = cross(velocity, b)
            for c in range(3):
                moved = field[c][r] + time_step * (push[c] - resist * j[c])
                field[c][r] = jnp.where(inside, moved, 0.0)
    for c in range(3):
        for r in range(2):
            pot_ref[c, r] = centre(field[c][r])
    pot_copy.start()
    mag_copy.wait()
    pot_copy.wait()


def relax(received, table_high, table_low, rows):
    shape = jax.ShapeDtypeStruct((3, 2, BAND, SECTOR), jnp.float32)
    vmem = pl.BlockSpec(memory_space=pltpu.VMEM)
    hbm = pl.BlockSpec(memory_space=pltpu.HBM)
    return pl.pallas_call(
        relax_kernel,
        out_shape=(shape, shape),
        in_specs=[vmem] * 4,
        out_specs=(hbm, hbm),
        scratch_shapes=[
            pltpu.VMEM((1024, 256), jnp.bfloat16),
            pltpu.VMEM((1024, 256), jnp.bfloat16),
            pltpu.VMEM((384, 256), jnp.float32),
            pltpu.VMEM((3, 144, 128), jnp.float32),
            pltpu.VMEM((3, 2, BAND, SECTOR), jnp.float32),
            pltpu.VMEM((3, 2, BAND, SECTOR), jnp.float32),
            pltpu.SemaphoreType.DMA((2,)),
        ],
        compiler_params=pltpu.CompilerParams(vmem_limit_bytes=40 * 1024 * 1024),
        name="relaxation",
    )(received, table_high, table_low, rows)


def per_device(coefficients, pair_orders):
    lat_pos = lax.axis_index("lat")
    lon_pos = lax.axis_index("lon")
    send = synthesize(pair_orders, coefficients).reshape(LAT, 1, CHUNKS * 128)
    half = lax.all_to_all(
        send, "lat", split_axis=0, concat_axis=0, tiled=True, axis_index_groups=[EXCHANGE]
    ).reshape(LAT * CHUNKS, 128)
    cores = [[2 * i, 2 * i + 1] for i in range(LON // 2)]
    received = lax.all_gather(half, "lon", axis=0, tiled=True, axis_index_groups=cores)

    by_pair = pair_orders.reshape(LAT, PAIRS_LOCAL)
    by_pair = by_pair.reshape(2, LAT_X, LAT_Z, PAIRS_LOCAL)[:, :, ::-1]
    by_pair = jnp.concatenate([by_pair[:, 2:], by_pair[:, :2]], axis=1).transpose(3, 0, 2, 1)
    by_pair = by_pair.reshape(PAIRS_LOCAL, LAT)
    orders = jnp.stack([by_pair, ORDERS - 1 - by_pair], axis=1).reshape(1, 512)
    orders = jnp.concatenate([orders, orders], axis=1)
    is_cos = jnp.arange(1024, dtype=jnp.int32)[None, :] < 512
    columns = jnp.arange(COLS, dtype=jnp.int32)[:, None]
    columns = lon_pos * SECTOR + jnp.where(columns < COLS - 8, columns, columns - COLS)
    turns = (orders * columns + jnp.where(is_cos, NP // 4, 0)) & (NP - 1)
    table = jnp.sin(turns.astype(jnp.float32) * (2.0 * math.pi / NP))
    rounded = lax.reduce_precision(table, exponent_bits=8, mantissa_bits=7)
    table_high = rounded.astype(jnp.bfloat16)
    table_low = (table - rounded).astype(jnp.bfloat16)

    row_ids = lat_pos * BAND - HALO + jnp.arange(EXT, dtype=jnp.int32)
    theta = span_start + (row_ids.astype(jnp.float32) + 0.5) * (span_width / NT)
    scale = 1.0 / (2.0 * (3.0 * NT / NP) * jnp.sin(theta))
    inside = ((row_ids >= 0) & (row_ids < NT)).astype(jnp.float32)
    rows = jnp.broadcast_to(jnp.stack([scale, inside])[:, :, None], (2, EXT, 128))
    return relax(received, table_high, table_low, rows)


def solution(mesh):
    in_specs = (P("lat", None, None, None, None), P())
    out_specs = (P(None, None, "lat", "lon"), P(None, None, "lat", "lon"))
    return jax.shard_map(
        per_device, mesh=mesh, in_specs=in_specs, out_specs=out_specs, check_vma=False
    )
```

```python
import math

import jax
import jax.numpy as jnp
import numpy as np
from jax import lax
from jax.experimental import pallas as pl
from jax.experimental.pallas import tpu as pltpu
from jax.sharding import PartitionSpec as P

ORDERS = 512
NT = 1024
NP = 2048
STEPS = 2
LAT = 64
LON = 8
BAND = NT // LAT
SECTOR = NP // LON
HALO = 4
EXT = BAND + 2 * HALO
PAIRS_LOCAL = 4
HALF = LAT // 2
CHUNKS = 9
COLS = SECTOR + 16

soft_floor = 1.0
resist = 0.2
time_step = 0.3
rescale_at = 1.0e10
block_steps = 16
span_start = math.pi / 6.0
span_width = 2.0 * math.pi / 3.0

LAT_X, LAT_Z = 4, 8
EXCHANGE = [
    y * HALF + (k + 2) % LAT_X * LAT_Z + z
    for y in range(2)
    for z in reversed(range(LAT_Z))
    for k in range(LAT_X)
]


def own_rows(core):
    first = [2 * core, 2 * core + 1, 4 + 2 * core, 5 + 2 * core]
    return first + [BAND - 1 - r for r in reversed(first)]


def geometry():
    own = np.array([own_rows(0), own_rows(1)])
    rows = BAND * np.arange(HALF)[None, None, :] + own[:, :, None]
    theta = span_start + (rows + 0.5) * (span_width / NT)
    cosine = np.tile(np.cos(theta), (1, 1, PAIRS_LOCAL))
    log_sin = np.tile(np.log(np.sin(theta)), (1, 1, PAIRS_LOCAL))
    return np.stack([cosine, log_sin], axis=1).astype(np.float32)


def norm_logs():
    k = np.arange(1, ORDERS, dtype=np.float64)
    logs = np.concatenate([[0.0], np.cumsum(0.5 * np.log((2 * k + 1) / (2 * k)))])
    return (logs - 0.5 * np.log(4 * np.pi)).astype(np.float32)


def split2(value):
    high = value.astype(jnp.bfloat16)
    low = (value - high.astype(jnp.float32)).astype(jnp.bfloat16)
    return high, low


def dot(a, b):
    return jnp.dot(a, b, preferred_element_type=jnp.float32)


def synth_kernel(
    order_hbm, log_hbm, geom_hbm, coef_hbm, out_ref,
    order_ref, log_ref, geom_ref, coef_ref, fac_ref, back_ref, leg_ref, coefs_ref, wh_ref, wl_ref, stack_ref,
    early_ref, sems,
):
    lat_pos = lax.axis_index("lat")
    core = lax.axis_index("lon") % 2
    copies = [
        pltpu.make_async_copy(order_hbm, order_ref, sems.at[0]),
        pltpu.make_async_copy(log_hbm, log_ref, sems.at[1]),
        pltpu.make_async_copy(geom_hbm.at[core], geom_ref, sems.at[2]),
        pltpu.make_async_copy(coef_hbm, coef_ref, sems.at[3]),
    ]
    for copy in copies:
        copy.start()
    coefs_ref[...] = jnp.zeros_like(coefs_ref)
    lane = lax.broadcasted_iota(jnp.int32, (8, 128), 1)
    pair_of_lane = lane // HALF

    def per_pair(values):
        result = jnp.full((8, 128), values[0], values[0].dtype)
        for p in range(1, PAIRS_LOCAL):
            result = jnp.where(pair_of_lane == p, values[p], result)
        return result

    copies[0].wait()
    lows = [order_ref[lat_pos * PAIRS_LOCAL + p] for p in range(PAIRS_LOCAL)]
    low = per_pair([o.astype(jnp.float32) for o in lows])
    high = (ORDERS - 1.0) - low
    switch = ORDERS - low

    def factors(c):
        step = lax.broadcasted_iota(jnp.int32, (8, 128), 0).astype(jnp.float32) + float(8 * c)
        if c < 32:
            order, degree = low, low + step
        else:
            low_side = step < switch
            order = jnp.where(low_side, low, high)
            degree = jnp.where(low_side, low + step, step - 1.0)
        prior = degree - 1.0
        order2 = order * order
        degree2 = degree * degree
        prior2 = prior * prior
        factor = jnp.sqrt(jnp.maximum(4.0 * degree2 - 1.0, 1.0) / jnp.maximum(degree2 - order2, 1.0))
        back = jnp.sqrt(jnp.maximum(prior2 - order2, 0.0) / jnp.maximum(4.0 * prior2 - 1.0, 1.0))
        if c >= 32:
            factor = jnp.where(degree > order, factor, 0.0)
        fac_ref[8 * c:8 * c + 8, :] = factor
        back_ref[8 * c:8 * c + 8, :] = jnp.where(prior > order, factor * back, 0.0)

    for c in range(32):
        factors(c)

    copies[1].wait()
    copies[2].wait()
    cosine = geom_ref[0]
    log_sin = geom_ref[1]
    norm_low = per_pair([log_ref[o] for o in lows])
    norm_high = per_pair([log_ref[ORDERS - 1 - o] for o in lows])
    seed_low = norm_low + low * log_sin
    seed_high = norm_high + high * log_sin
    start_scale = jnp.exp(seed_high)
    log_big = math.log(rescale_at)

    def run(base, count, state, restart, first):
        previous, current, scaling, scale = state
        for k in range(count):
            s = base + k
            fac = fac_ref[pl.ds(s, 1), :]
            back = back_ref[pl.ds(s, 1), :]
            from_previous = back * previous
            if restart:
                starting = switch == (s.astype(jnp.float32) if not isinstance(s, int) else float(s))
                scaling = jnp.where(starting, seed_high, scaling)
                scale = jnp.where(starting, start_scale, scale)
                value = (fac * cosine) * current + (jnp.where(starting, 1.0, 0.0) - from_previous)
            elif first and k == 0:
                value = jnp.ones((8, 128), jnp.float32)
            else:
                value = (fac * cosine) * current - from_previous
            previous, current = current, value
            at = s * 8 if isinstance(s, int) else pl.multiple_of(s * 8, 8)
            leg_ref[pl.ds(at, 8), :] = value * scale
        big = jnp.abs(current) > rescale_at
        shrink = jnp.where(big, 1.0 / rescale_at, 1.0)
        scaling = scaling + jnp.where(big, log_big, 0.0)
        return previous * shrink, current * shrink, scaling, jnp.exp(scaling)

    zero = jnp.zeros((8, 128), jnp.float32)
    state = (zero, zero, seed_low, jnp.exp(seed_low))
    for b in range(16):
        state = run(b * block_steps, block_steps, state, False, b == 0)
        factors(32 + 2 * b)
        factors(33 + 2 * b)
    factors(64)
    copies[3].wait()
    for p in range(PAIRS_LOCAL):
        for x in range(2):
            for c in range(3):
                row = (p * 2 + x) * 8 + c * 2
                coefs_ref[row:row + 2, 0:513] = coef_ref[p, x, c]
    slot = lax.broadcasted_iota(jnp.int32, (8, 512), 1)
    for p in range(PAIRS_LOCAL):
        is_low = slot < ORDERS - lows[p]
        low_sign = 1.0 - 2.0 * (slot % 2).astype(jnp.float32)
        high_sign = 1.0 - 2.0 * ((slot + lows[p]) % 2).astype(jnp.float32)
        for x in range(2):
            row = (p * 2 + x) * 8
            both = coefs_ref[row:row + 8, 0:512]
            parts = [jnp.where(is_low, both, 0.0), jnp.where(is_low, 0.0, both)]
            for side in range(2):
                for h in range(2):
                    w = parts[h] if side == 0 else parts[h] * (low_sign if h == 0 else high_sign)
                    at = (((h * 2 + side) * PAIRS_LOCAL + p) * 2 + x) * 8
                    wh, wl = split2(w)
                    wh_ref[at:at + 8, :] = wh.astype(jnp.float32)
                    wl_ref[at:at + 8, :] = wl.astype(jnp.float32)

    tail_sign = per_pair([1.0 - 2.0 * (o % 2).astype(jnp.float32) for o in lows])
    tails = []
    for x in range(2):
        tail = jnp.zeros((8, 128), jnp.float32)
        for p in range(PAIRS_LOCAL):
            row = (p * 2 + x) * 8
            column = jnp.broadcast_to(coefs_ref[row:row + 8, 512:513], (8, 128))
            tail = jnp.where(pair_of_lane == p, column, tail)
        tails.append(tail)

    def contract(t0, half):
        at = 256 * half
        values = jnp.concatenate(
            [leg_ref[pl.ds(8 * at + t0 + d, 256, stride=8), :] for d in range(2)], axis=1
        )
        vh, vl = split2(values)
        rows = 256 if half == 1 else 128
        wh = wh_ref[0:rows, at:at + 256].astype(jnp.bfloat16)
        wl = wl_ref[0:rows, at:at + 256].astype(jnp.bfloat16)
        summed = dot(wh, vh) + dot(wl, vh) + dot(wh, vl)
        for d in range(2):
            t = t0 + d
            part = summed[:, 128 * d:128 * d + 128]
            if half == 1:
                last = leg_ref[pl.ds(512 * 8 + t, 1), :]
            for side in range(2):
                for h in range(2 if half == 1 else 1):
                    for x in range(2):
                        picked = None
                        for p in range(PAIRS_LOCAL):
                            row = (((h * 2 + side) * PAIRS_LOCAL + p) * 2 + x) * 8
                            block = part[row:row + 8, :]
                            picked = block if p == 0 else jnp.where(pair_of_lane == p, block, picked)
                        q = 2 + (t if side == 0 else 7 - t)
                        which = (side * 2 + h) * 2 + x
                        if h == 0:
                            keep = (side * 2 + x) * 8 + t
                            if half == 0:
                                early_ref[keep] = picked
                                continue
                            picked = picked + early_ref[keep]
                        else:
                            term = tails[x] * last
                            picked = picked + (term if side == 0 else term * tail_sign)
                        stack_ref[which, 6 * q:6 * q + 6, :] = picked[0:6]

    for part in range(4):
        for b in range(4):
            state = run((16 + 4 * part + b) * block_steps, block_steps, state, True, False)
        contract(2 * part, 0)
    run(512, 1, state, True, False)
    for part in range(4):
        contract(2 * part, 1)

    unit = lax.broadcasted_iota(jnp.int32, (12, 128), 1) % HALF
    for h in range(2):
        for x in range(2):
            north, south = h * 2 + x, 4 + h * 2 + x
            n_first, n_last = stack_ref[north, 12:24, :], stack_ref[north, 48:60, :]
            s_first, s_last = stack_ref[south, 12:24, :], stack_ref[south, 48:60, :]
            stack_ref[north, 0:12, :] = jnp.where(unit == 0, 0.0, pltpu.roll(n_last, 1, 1))
            stack_ref[north, 60:72, :] = jnp.where(unit == HALF - 1, s_first, pltpu.roll(n_first, 127, 1))
            stack_ref[south, 0:12, :] = jnp.where(unit == HALF - 1, n_last, pltpu.roll(s_last, 127, 1))
            stack_ref[south, 60:72, :] = jnp.where(unit == 0, 0.0, pltpu.roll(s_first, 1, 1))

    group = lax.broadcasted_iota(jnp.int32, (HALF, 128), 1) // HALF
    wide = lax.broadcasted_iota(jnp.int32, (128, 128), 1)
    x, z = (wide + 2) % LAT_X, (wide // LAT_X) % LAT_Z
    base = wide // HALF * HALF
    source = [base + x * LAT_Z + (LAT_Z - 1 - z), base + (LAT_X - 1 - x) * LAT_Z + z]

    def by_member(value, side):
        return jnp.take_along_axis(value, source[side], axis=1)

    for side in range(2):
        for h in range(2):
            which = (side * 2 + h) * 2
            turned = by_member(
                jnp.concatenate([stack_ref[which, 0:64, :], stack_ref[which + 1, 0:64, :]], axis=0), side
            ).T
            for p in range(PAIRS_LOCAL):
                out_ref[pl.ds(side * HALF * CHUNKS + p * 2 + h, HALF, stride=CHUNKS), :] = turned[
                    HALF * p:HALF * p + HALF, :
                ]
        rest = jnp.concatenate([stack_ref[side * 4 + k, 64:72, :] for k in range(4)] * PAIRS_LOCAL, axis=0)
        rest = by_member(rest, side).T
        picked = rest[0:HALF, :]
        for p in range(1, PAIRS_LOCAL):
            picked = jnp.where(group == p, rest[HALF * p:HALF * p + HALF, :], picked)
        out_ref[pl.ds(side * HALF * CHUNKS + 8, HALF, stride=CHUNKS), :] = picked


def synthesize(pair_orders, coefficients):
    hbm = pl.BlockSpec(memory_space=pltpu.HBM)
    scratch = [
        pltpu.SMEM((256,), jnp.int32),
        pltpu.SMEM((512,), jnp.float32),
        pltpu.VMEM((2, 8, 128), jnp.float32),
        pltpu.VMEM((4, 2, 3, 2, 513), jnp.float32),
        pltpu.VMEM((520, 128), jnp.float32),
        pltpu.VMEM((520, 128), jnp.float32),
        pltpu.VMEM((520 * 8, 128), jnp.float32),
        pltpu.VMEM((64, 640), jnp.float32),
        pltpu.VMEM((256, 512), jnp.float32),
        pltpu.VMEM((256, 512), jnp.float32),
        pltpu.VMEM((8, 72, 128), jnp.float32),
        pltpu.VMEM((32, 8, 128), jnp.float32),
        pltpu.SemaphoreType.DMA((4,)),
    ]
    return pl.pallas_call(
        synth_kernel,
        out_shape=jax.ShapeDtypeStruct((LAT * CHUNKS, 128), jnp.float32),
        in_specs=[hbm] * 4,
        out_specs=pl.BlockSpec(memory_space=pltpu.VMEM),
        scratch_shapes=scratch,
        compiler_params=pltpu.CompilerParams(vmem_limit_bytes=60 * 1024 * 1024),
        name="synthesis",
    )(pair_orders, norm_logs(), geometry(), coefficients)


def relax_kernel(
    recv_ref, th_ref, tl_ref, pot_hbm, mag_hbm, dh_ref, dl_ref, turn_ref, plane_ref, pot_ref, mag_ref, sems
):
    lane = lax.broadcasted_iota(jnp.int32, (LAT, 128), 1)
    for half in range(2):
        start = half * LAT * CHUNKS
        at = half * 128
        rest = recv_ref[pl.ds(start + 8, LAT, stride=CHUNKS), :]
        crossed = pltpu.roll(rest, 64, 1)
        for both in range(8):
            main = recv_ref[pl.ds(start + both, LAT, stride=CHUNKS), :]
            for x in range(2):
                ox = both * 2 + x
                side = 1 - x
                tail = rest if (ox >= 8) == (side == 1) else crossed
                tail = jnp.where(lane // 8 == side * 8 + ox % 8, tail, 0.0)
                value = jnp.where(lane < 64, main, tail) if x == 0 else jnp.where(lane < 64, tail, main)
                high, low = split2(value)
                row = (x * 8 + both) * LAT
                dh_ref[row:row + LAT, at:at + 128] = high
                dl_ref[row:row + LAT, at:at + 128] = low
    parts = []
    for x in range(2):
        k = slice(512 * x, 512 * x + 512)
        dh, dl, th, tl = dh_ref[k, :], dl_ref[k, :], th_ref[:, k], tl_ref[:, k]
        parts.append(dot(th, dh) + dot(tl, dh) + dot(th, dl))
    for half in range(2):
        block = slice(128 * half, 128 * half + 128)
        summed = parts[0][:, block] + pltpu.roll(parts[1][:, block], 64, 1)
        turn_ref[0:COLS - 8, block] = summed[0:COLS - 8]
        turn_ref[376:384, block] = summed[COLS - 8:COLS]
    turn_ref[COLS - 8:376, :] = jnp.zeros((384 - COLS, 256), jnp.float32)
    for j in range(3):
        for half in range(2):
            turned = turn_ref[128 * j:128 * j + 128, 128 * half:128 * half + 128].T
            tail = turned[64:72, :]
            for g in range(1, 8):
                tail = tail + turned[64 + 8 * g:72 + 8 * g, :]
            turned = jnp.concatenate([turned[0:64, :], tail], axis=0)
            starts = [2 - 2 * half] + [HALO + r for r in own_rows(half)[::2]] + [20 + 2 * half]
            for k, e in enumerate(starts):
                plane_ref[j, 6 * e:6 * e + 12, :] = turned[12 * k:12 * k + 12, :]
    planes = [
        jnp.concatenate([plane_ref[j, pl.ds(cr, EXT, stride=6), :] for j in range(3)], axis=1)
        for cr in range(6)
    ]
    field = [[planes[c * 2 + r] for r in range(2)] for c in range(3)]
    row_ids = lax.broadcasted_iota(jnp.int32, (EXT, 128), 0) + (lax.axis_index("lat") * BAND - HALO)
    theta = span_start + (row_ids.astype(jnp.float32) + 0.5) * (span_width / NT)
    scale = jnp.concatenate([1.0 / (2.0 * (3.0 * NT / NP) * jnp.sin(theta))] * 3, axis=1)
    row_ids = jnp.concatenate([row_ids] * 3, axis=1)
    inside = (row_ids >= 0) & (row_ids < NT)

    def d_theta(a):
        return 0.5 * (pltpu.roll(a, EXT - 1, 0) - pltpu.roll(a, 1, 0))

    def d_phi(a):
        return (pltpu.roll(a, 383, 1) - pltpu.roll(a, 1, 1)) * scale

    def d_rad(pair):
        return [0.5 * pair[1], -0.5 * pair[0]]

    def curl(f):
        rad, colat, lon = f
        lon_r, colat_r = d_rad(lon), d_rad(colat)
        return [
            [d_theta(lon[r]) - d_phi(colat[r]) for r in range(2)],
            [d_phi(rad[r]) - lon_r[r] for r in range(2)],
            [colat_r[r] - d_theta(rad[r]) for r in range(2)],
        ]

    def cross(a, b):
        return [a[1] * b[2] - a[2] * b[1], a[2] * b[0] - a[0] * b[2], a[0] * b[1] - a[1] * b[0]]

    def centre(a):
        return pltpu.roll(a[:, 0:SECTOR], EXT - HALO, 0)[0:BAND]

    pot_copy = pltpu.make_async_copy(pot_ref, pot_hbm, sems.at[0])
    mag_copy = pltpu.make_async_copy(mag_ref, mag_hbm, sems.at[1])
    for step in range(STEPS):
        magnetic = [[jnp.where(inside, b, 0.0) for b in pair] for pair in curl(field)]
        if step == STEPS - 1:
            for c in range(3):
                for r in range(2):
                    mag_ref[c, r] = centre(magnetic[c][r])
            mag_copy.start()
        current = curl(magnetic)
        for r in range(2):
            b = [magnetic[c][r] for c in range(3)]
            j = [current[c][r] for c in range(3)]
            weight = 1.0 / (b[0] * b[0] + b[1] * b[1] + b[2] * b[2] + soft_floor)
            velocity = [f * weight for f in cross(j, b)]
            push = cross(velocity, b)
            for c in range(3):
                moved = field[c][r] + time_step * (push[c] - resist * j[c])
                field[c][r] = jnp.where(inside, moved, 0.0)
    for c in range(3):
        for r in range(2):
            pot_ref[c, r] = centre(field[c][r])
    pot_copy.start()
    mag_copy.wait()
    pot_copy.wait()


def relax(received, table_high, table_low):
    shape = jax.ShapeDtypeStruct((3, 2, BAND, SECTOR), jnp.float32)
    vmem = pl.BlockSpec(memory_space=pltpu.VMEM)
    hbm = pl.BlockSpec(memory_space=pltpu.HBM)
    return pl.pallas_call(
        relax_kernel,
        out_shape=(shape, shape),
        in_specs=[vmem] * 3,
        out_specs=(hbm, hbm),
        scratch_shapes=[
            pltpu.VMEM((1024, 256), jnp.bfloat16),
            pltpu.VMEM((1024, 256), jnp.bfloat16),
            pltpu.VMEM((384, 256), jnp.float32),
            pltpu.VMEM((3, 144, 128), jnp.float32),
            pltpu.VMEM((3, 2, BAND, SECTOR), jnp.float32),
            pltpu.VMEM((3, 2, BAND, SECTOR), jnp.float32),
            pltpu.SemaphoreType.DMA((2,)),
        ],
        compiler_params=pltpu.CompilerParams(vmem_limit_bytes=40 * 1024 * 1024),
        name="relaxation",
    )(received, table_high, table_low)


def per_device(coefficients, pair_orders):
    lon_pos = lax.axis_index("lon")
    send = synthesize(pair_orders, coefficients).reshape(LAT, 1, CHUNKS * 128)
    half = lax.all_to_all(
        send, "lat", split_axis=0, concat_axis=0, tiled=True, axis_index_groups=[EXCHANGE]
    ).reshape(LAT * CHUNKS, 128)
    cores = [[2 * i, 2 * i + 1] for i in range(LON // 2)]
    received = lax.all_gather(half, "lon", axis=0, tiled=True, axis_index_groups=cores)

    by_pair = pair_orders.reshape(LAT, PAIRS_LOCAL)
    by_pair = by_pair.reshape(2, LAT_X, LAT_Z, PAIRS_LOCAL)[:, :, ::-1]
    by_pair = jnp.concatenate([by_pair[:, 2:], by_pair[:, :2]], axis=1).transpose(3, 0, 2, 1)
    by_pair = by_pair.reshape(PAIRS_LOCAL, LAT)
    orders = jnp.stack([by_pair, ORDERS - 1 - by_pair], axis=1).reshape(1, 512)
    orders = jnp.concatenate([orders, orders], axis=1)
    is_cos = jnp.arange(1024, dtype=jnp.int32)[None, :] < 512
    columns = jnp.arange(COLS, dtype=jnp.int32)[:, None]
    columns = lon_pos * SECTOR + jnp.where(columns < COLS - 8, columns, columns - COLS)
    turns = (orders * columns + jnp.where(is_cos, NP // 4, 0)) & (NP - 1)
    table = jnp.sin(turns.astype(jnp.float32) * (2.0 * math.pi / NP))
    rounded = lax.reduce_precision(table, exponent_bits=8, mantissa_bits=7)
    table_high = rounded.astype(jnp.bfloat16)
    table_low = (table - rounded).astype(jnp.bfloat16)

    return relax(received, table_high, table_low)


def solution(mesh):
    in_specs = (P("lat", None, None, None, None), P())
    out_specs = (P(None, None, "lat", "lon"), P(None, None, "lat", "lon"))
    return jax.shard_map(
        per_device, mesh=mesh, in_specs=in_specs, out_specs=out_specs, check_vma=False
    )
```
